256 devices in a mesh: tm: 32 (over y, z), weight: 8 (over x, core).
Axes of the slice: x: 4, y: 4, z: 8, core: 2. Of those that a mesh axis runs over, the one named last changes fastest.
Arguments:
- tokens: bfloat16 [32768, 2560], P(('tm', 'weight')), may hold values from -6 to 6
- segments: int32 [32768], P('tm'), may hold values from 0 to 31, never falling along the last dimension, each value on 1 to 3072 neighbouring positions
- w_z: bfloat16 [2560, 3072], P(None, 'weight'), may hold values from -0.125 to 0.125
- w_x: bfloat16 [2560, 3072], P(None, 'weight'), may hold values from -0.125 to 0.125
- w_dt: bfloat16 [2560, 48], P(None, 'weight'), may hold values from -0.125 to 0.125
- w_bc: bfloat16 [2560, 256], replicated, may hold values from -0.125 to 0.125
- conv_x: float32 [4, 3072], P(None, 'weight'), may hold values from -2.5 to 2.5
- conv_bc: float32 [4, 256], replicated, may hold values from -2.5 to 2.5
- dt_bias: float32 [48], P('weight'), may hold values from -3 to -1
- decay_rate: float32 [48], P('weight'), may hold values from 0 to 1.5
- skip_d: float32 [48], P('weight'), may hold values from 0.5 to 1.5
- norm_gain: bfloat16 [3072], P('weight'), may hold values from 0.5 to 1.5
- w_out: bfloat16 [3072, 2560], P('weight'), may hold values from -0.109375 to 0.109375
Outputs:
- mixed: bfloat16 [32768, 2560], P(('tm', 'weight'))
The draws below stay inside these ranges and needn't reach their ends.
Inputs may be any that keep to these rules, and one draw needn't show every extreme that they name: `segments`: document numbers never fall along the stream; a document has at most 3072 frames.
All inputs are finite; a program needn't handle non-finite values.
Results may differ from the reference program's by a relative error of at most 0.015.
Values may be sent and summed in bfloat16 or wider, within the bound.
A program may use at most 64 MiB of HBM per device.

```python
import math
import jax
import jax.numpy as jnp
import numpy as np
from jax import lax

D = 2560
HEADS = 48
STATE = 128
GROUP = 256
DI = 3072
BLOCK = 1024
TOKENS = 32768
N_TM = 32


def draw_decay_rate(key, part):
    length = TOKENS * 1.0
    pick = jax.random.uniform(jax.random.fold_in(key, 11), (HEADS,), jnp.float32)
    return jnp.exp(jnp.log(1.0 / length) + pick * jnp.log(length))


def block_scale(own_key, extent, pieces, least, high):
    loudness, own = 1.0, jax.random.fold_in(own_key, 6)
    for position, parts in pieces:
        draws = jnp.exp(jax.random.uniform(jax.random.fold_in(own, position), (parts,), jnp.float32, least / len(pieces), high / len(pieces)))
        loudness = loudness * jnp.repeat(draws, extent[position] // parts).reshape([-1 if axis == position else 1 for axis in range(len(extent))])
    return loudness


def length_profile(number_of, total, bound, skew):
    weights = [(1 << 20) // math.isqrt(standing ** skew) + 1 for standing in range(2, number_of + 1)]
    spare, given = total - bound - (number_of - 1), [1] * (number_of - 1)
    while spare > 0:
        free = [i for i in range(number_of - 1) if given[i] < bound]
        mass, left = sum([weights[i] for i in free]), spare
        for i in free:
            extra = min(bound - given[i], max(1, left * weights[i] // mass), spare)
            given[i] = given[i] + extra
            spare = spare - extra
    return np.array([bound] + given)


def uneven_parts(own_key, number_of, total, bound, skew):
    if number_of == 2:
        one = jax.random.randint(own_key, (), max(1, total - bound), min(bound, total - 1) + 1)
        return jnp.stack([one, total - one])
    lengths = jnp.asarray(length_profile(number_of, total, bound, skew), jnp.int32)
    twos = (number_of - 1) // 2
    giver, sink = lengths[1:1 + 2 * twos:2], lengths[2:2 + 2 * twos:2]
    slack = jnp.minimum(giver - 1, bound - sink)
    shifted = jax.random.randint(jax.random.fold_in(own_key, 1), (twos,), 0, 1 << 20) % (slack + 1)
    lengths = lengths.at[1:1 + 2 * twos:2].set(giver - shifted).at[2:2 + 2 * twos:2].set(sink + shifted)
    return lengths[jax.random.permutation(jax.random.fold_in(own_key, 2), number_of)]


def normal_values(own_key, extent, scale, most, cuts=(), dtype=jnp.bfloat16):
    values = scale * jax.random.normal(own_key, extent, jnp.float32)
    if cuts:
        values = values * block_scale(own_key, extent, cuts, -0.22, 0.18)
    return jnp.clip(values, -most, most).astype(dtype)


def setup_inputs(seed: int = 0) -> dict:
    key_list = jax.random.split(jax.random.key(seed), 14)
    tokens = normal_values(key_list[0], (TOKENS, D), 1.0, 6.0, ((0, 256),))
    segments = jnp.searchsorted(jnp.cumsum(uneven_parts(key_list[1], N_TM, TOKENS, 3 * BLOCK, 1)), jnp.arange(TOKENS), side="right").astype(jnp.int32)
    w_z = normal_values(key_list[2], (D, DI), D ** -0.5, 0.125, ((1, 8),))
    w_x = normal_values(key_list[3], (D, DI), D ** -0.5, 0.125, ((1, 8),))
    w_dt = normal_values(key_list[4], (D, HEADS), D ** -0.5, 0.125, ((1, 8),))
    w_bc = normal_values(key_list[5], (D, 2 * STATE), D ** -0.5, 0.125)
    conv_x = normal_values(key_list[6], (4, DI), 0.5, 2.5, ((1, 8),), jnp.float32)
    conv_bc = normal_values(key_list[7], (4, 2 * STATE), 0.5, 2.5, (), jnp.float32)
    dt_bias = jnp.clip(-3.0 + 2.0 * jax.random.uniform(key_list[8], (HEADS,), jnp.float32) ** block_scale(key_list[8], (HEADS,), ((0, 8),), -0.2, 0.2), -3.0, -1.0)
    decay_rate = draw_decay_rate(jax.random.fold_in(key_list[13], 71), 0)
    skip_d = jnp.clip(0.5 + 1.0 * jax.random.uniform(key_list[10], (HEADS,), jnp.float32) ** block_scale(key_list[10], (HEADS,), ((0, 8),), -0.2, 0.2), 0.5, 1.5)
    norm_gain = jnp.clip(1.0 + 0.1 * jax.random.normal(key_list[11], (DI,), jnp.float32), 0.5, 1.5).astype(jnp.bfloat16)
    w_out = normal_values(key_list[12], (DI, D), DI ** -0.5, 0.109375, ((0, 8),))
    return {"tokens": tokens, "segments": segments, "w_z": w_z, "w_x": w_x, "w_dt": w_dt, "w_bc": w_bc, "conv_x": conv_x, "conv_bc": conv_bc, "dt_bias": dt_bias, "decay_rate": decay_rate, "skip_d": skip_d, "norm_gain": norm_gain, "w_out": w_out}


eps_norm = 1e-05

def conv_rows(xbc, seg, prev_xbc, prev_seg, conv_w):
    full = jnp.concatenate([prev_xbc, xbc], 0).astype(jnp.float32)
    segs = jnp.concatenate([prev_seg, seg], 0)
    count = xbc.shape[0]
    total = jnp.zeros(xbc.shape, jnp.float32)
    for k in range(4):
        same = (segs[k:k + count] == seg).astype(jnp.float32)
        total = total + full[k:k + count] * conv_w[k][None, :] * same[:, None]
    return jax.nn.silu(total)

def group_ssd(xs, dts, rate, bmat, cmat, seg, ssm, seg_in):
    size = seg.shape[0]
    logs = jnp.cumsum(-dts * rate[None, :], axis=0)
    order = jnp.arange(size)
    lower = (order[:, None] >= order[None, :]) & (seg[:, None] == seg[None, :])
    scores = jnp.dot(cmat, bmat.T, preferred_element_type=jnp.float32)
    diff = jnp.minimum(logs[:, None, :] - logs[None, :, :], 0.0)
    mix = jnp.where(lower[:, :, None], jnp.exp(diff), 0.0) * scores[:, :, None] * dts[None, :, :]
    mix = mix.astype(jnp.bfloat16)
    inner = jnp.einsum('ijh,jhp->ihp', mix.astype(jnp.float32), xs.astype(jnp.float32))
    enter = jnp.exp(logs) * (seg == seg_in).astype(jnp.float32)[:, None]
    carried = jnp.einsum('in,hnp->ihp', cmat.astype(jnp.float32), ssm, precision=lax.Precision.HIGHEST) * enter[:, :, None]
    tail = jnp.exp(logs[-1][None, :] - logs) * (seg == seg[-1]).astype(jnp.float32)[:, None] * dts
    scaled = (xs.astype(jnp.float32) * tail[:, :, None]).astype(jnp.bfloat16)
    fresh = jnp.einsum('jn,jhp->hnp', bmat.astype(jnp.float32), scaled.astype(jnp.float32))
    keep = jnp.exp(logs[-1]) * (seg[-1] == seg_in).astype(jnp.float32)
    return (inner + carried, ssm * keep[:, None, None] + fresh)

def reference(tokens, segments, w_z, w_x, w_dt, w_bc, conv_x, conv_bc, dt_bias, decay_rate, skip_d, norm_gain, w_out):
    width = w_x.shape[1]
    heads = decay_rate.shape[0]
    head_dim = width // heads
    state = w_bc.shape[1] // 2
    panel = jnp.concatenate([w_z, w_x, w_bc, w_dt], axis=1)
    conv_w = jnp.concatenate([conv_x, conv_bc], axis=1)
    count = tokens.shape[0] // GROUP
    tok_blocks = tokens.reshape(count, GROUP, tokens.shape[1])
    seg_blocks = segments.reshape(count, GROUP)
    gain = norm_gain.astype(jnp.float32)

    def advance(carry, inputs):
        ssm, seg_in, prev_xbc, prev_seg = carry
        rows, seg = inputs
        proj = jnp.dot(rows, panel, preferred_element_type=jnp.float32).astype(jnp.bfloat16)
        gate_z = proj[:, :width]
        xbc = proj[:, width:2 * width + 2 * state]
        dt_raw = proj[:, 2 * width + 2 * state:]
        conv = conv_rows(xbc, seg, prev_xbc, prev_seg, conv_w).astype(jnp.bfloat16)
        xs = conv[:, :width].reshape(GROUP, heads, head_dim)
        bmat = conv[:, width:width + state]
        cmat = conv[:, width + state:]
        dts = jax.nn.softplus(dt_raw.astype(jnp.float32) + dt_bias[None, :])
        ys, ssm_next = group_ssd(xs, dts, decay_rate, bmat, cmat, seg, ssm, seg_in)
        ys = ys + skip_d[None, :, None] * xs.astype(jnp.float32)
        gated = ys.reshape(GROUP, width) * jax.nn.silu(gate_z.astype(jnp.float32))
        inverse = lax.rsqrt(lax.optimization_barrier(jnp.mean(gated * gated, axis=1)) + eps_norm)
        normed = (gated * inverse[:, None] * gain[None, :]).astype(jnp.bfloat16)
        result = jnp.dot(normed, w_out, preferred_element_type=jnp.float32).astype(jnp.bfloat16)
        return ((ssm_next, seg[-1], xbc[-3:], seg[-3:]), result)
    start = (jnp.zeros((heads, state, head_dim), jnp.float32), jnp.zeros((), jnp.int32), jnp.zeros((3, width + 2 * state), jnp.bfloat16), jnp.zeros((3,), jnp.int32))
    final, outputs = lax.scan(advance, start, (tok_blocks, seg_blocks))
    return outputs.reshape(tokens.shape[0], tokens.shape[1])
```

```python
import functools

import jax
import jax.numpy as jnp
from jax import lax
from jax.experimental import pallas as pl
from jax.experimental.pallas import tpu as pltpu
from jax.sharding import PartitionSpec as P

GROUP = 256
LANES = 128
HALO = 16
EPS = 1e-5
F32 = jnp.float32
BF16 = jnp.bfloat16
MESH = pl.DeviceIdType.MESH
VMEM_LIMIT = 60 * 1024 * 1024


def whole(space=pltpu.VMEM):
    return pl.BlockSpec(memory_space=space)


def here():
    w = lax.axis_index("weight")
    return lax.axis_index("tm"), lax.div(w, 2), lax.rem(w, 2)


def at(t, x, c):
    return {"tm": t, "weight": x * 2 + c}


def greet(senders, receivers_count):
    barrier = pltpu.get_barrier_semaphore()
    for device in senders:
        pl.semaphore_signal(barrier, inc=1, device_id=device, device_id_type=MESH)
    pl.semaphore_wait(barrier, receivers_count)


def remote(src, dst, send, recv, device):
    return pltpu.make_async_remote_copy(
        src_ref=src, dst_ref=dst, send_sem=send, recv_sem=recv, device_id=device, device_id_type=MESH
    )


def mm(a, b):
    return jnp.dot(a, b, preferred_element_type=F32)


def gather_kernel(
    nx, nt, tok, seg, wz, wx, wbc, wdt, wo,
    z_out, xbc_out, dt_out, halo_out, seg_out, wo_out,
    buf, wzx_v, wbc_v, wdt_v, halo_s, seg_s, send, recv, local,
):
    t, x, c = here()
    rows = tok.shape[0]
    half = rows // 2
    width = wz.shape[1]
    right = at(t, lax.rem(x + 1, nx), c)
    left = at(t, lax.rem(x + nx - 1, nx), c)
    mate = at(t, x, 1 - c)
    after = at(lax.rem(t + 1, nt), x, c)
    before = at(lax.rem(t + nt - 1, nt), x, c)

    def chunk(xx, cc, start=0, size=rows):
        begin = (lax.rem(xx + nx, nx) * 2 + cc) * rows + start
        return buf.at[pl.ds(pl.multiple_of(begin, half), size)]

    own = pltpu.make_async_copy(tok, chunk(x, c), local.at[0])
    own.start()
    greet((right, left, mate, before), 4)
    r0 = remote(tok.at[pl.ds(0, half)], chunk(x, c, 0, half), send.at[0], recv.at[0], right)
    r1 = remote(tok.at[pl.ds(half, half)], chunk(x, c, half, half), send.at[1], recv.at[1], right)
    l1 = remote(tok.at[pl.ds(half, half)], chunk(x, c, half, half), send.at[2], recv.at[2], left)
    l0 = remote(tok.at[pl.ds(0, half)], chunk(x, c, 0, half), send.at[3], recv.at[3], left)
    m0 = remote(tok, chunk(x, c), send.at[4], recv.at[4], mate)
    m0.start()
    r0.start()
    l1.start()
    r1.start()
    l0.start()
    loads = [
        pltpu.make_async_copy(wz, wzx_v.at[:, pl.ds(0, width)], local.at[1]),
        pltpu.make_async_copy(wx, wzx_v.at[:, pl.ds(width, width)], local.at[2]),
        pltpu.make_async_copy(wbc, wbc_v, local.at[3]),
    ]
    for load in loads:
        load.start()
    to_seg = remote(seg, seg_s, send.at[11], recv.at[11], after)
    to_seg.start()
    to_wo = remote(wo, wo_out, send.at[12], recv.at[12], mate)
    to_wo.start()
    r2 = remote(chunk(x - 1, c, 0, half), chunk(x - 1, c, 0, half), send.at[5], recv.at[5], right)
    l2 = remote(chunk(x + 1, c, half, half), chunk(x + 1, c, half, half), send.at[6], recv.at[6], left)
    m1 = remote(chunk(x - 1, c), chunk(x - 1, c), send.at[7], recv.at[7], mate)
    m2 = remote(chunk(x + 1, c), chunk(x + 1, c), send.at[8], recv.at[8], mate)
    m3 = remote(chunk(x + 2, c), chunk(x + 2, c), send.at[9], recv.at[9], mate)
    last = xbc_out.shape[0] - HALO
    to_halo = remote(xbc_out.at[pl.ds(last, HALO)], halo_s, send.at[10], recv.at[10], after)

    wdt_v[...] = jnp.zeros_like(wdt_v)
    wdt_v[pl.ds(0, wdt.shape[0]), :] = wdt[...]

    def step(s, carry):
        @pl.when(s == 0)
        def _():
            own.wait()
            for load in loads:
                load.wait()
            m0.wait_recv()

        @pl.when(s == 1)
        def _():
            r0.wait_recv()
            r2.start()
            l1.wait_recv()
            l2.start()
            r1.wait_recv()
            m1.start()
            l0.wait_recv()
            m2.start()
            m1.wait_recv()

        @pl.when(s == 2)
        def _():
            m2.wait_recv()

        @pl.when(s == 3)
        def _():
            r2.wait_recv()
            l2.wait_recv()
            m3.start()
            m3.wait_recv()

        offset = jnp.where(s == 1, nx - 1, jnp.where(s == 2, 1, jnp.where(s == 3, 2, 0)))
        g = lax.rem(x + offset, nx)
        mine = pl.ds(pl.multiple_of(g * 2 * rows, 2 * rows), 2 * rows)
        v = mm(buf[mine, :], wbc_v[...]).astype(BF16)
        xbc_out[mine, pl.ds(width, 256)] = v
        v = mm(buf[mine, :], wzx_v[:, pl.ds(512, 256)]).astype(BF16)
        xbc_out[mine, pl.ds(128, 256)] = v
        v = mm(buf[mine, :], wzx_v[:, pl.ds(256, 256)]).astype(BF16)
        z_out[mine, pl.ds(256, 128)] = v[:, :128]
        xbc_out[mine, pl.ds(0, 128)] = v[:, 128:]
        v = mm(buf[mine, :], wzx_v[:, pl.ds(0, 256)]).astype(BF16)
        z_out[mine, pl.ds(0, 256)] = v
        v = lax.dot_general(
            buf[mine, :], wdt_v[...], (((1,), (1,)), ((), ())), preferred_element_type=F32
        )
        dt_out[mine, :] = v.astype(BF16).astype(F32)

        @pl.when(g == nx - 1)
        def _():
            to_halo.start()

        return carry

    lax.fori_loop(0, 4, step, 0)
    to_seg.wait_recv()
    seg_out[...] = seg_s[...]
    to_halo.wait_recv()
    halo_out[...] = halo_s[...]
    to_wo.wait_recv()
    for copy in (r0, r1, l1, l0, m0, r2, l2, m1, m2, m3, to_halo, to_seg, to_wo):
        copy.wait_send()


def gather_project(nx, nt, tokens, seg, w_z, w_x, w_bc, w_dt, w_out):
    rows, depth = tokens.shape
    width = w_z.shape[1]
    total = rows * nx * 2
    wide = width + w_bc.shape[1]
    hbm = whole(pl.ANY)
    return pl.pallas_call(
        functools.partial(gather_kernel, nx, nt),
        out_shape=(
            jax.ShapeDtypeStruct((total, width), BF16),
            jax.ShapeDtypeStruct((total, wide), BF16),
            jax.ShapeDtypeStruct((total, LANES), F32),
            jax.ShapeDtypeStruct((HALO, wide), BF16),
            jax.ShapeDtypeStruct(seg.shape, jnp.int32),
            jax.ShapeDtypeStruct(w_out.shape, BF16),
        ),
        in_specs=[hbm, whole(), hbm, hbm, hbm, whole(), hbm],
        out_specs=(whole(), whole(), whole(), whole(), whole(), hbm),
        scratch_shapes=[
            pltpu.VMEM((total, depth), BF16),
            pltpu.VMEM((depth, 2 * width), BF16),
            pltpu.VMEM((depth, w_bc.shape[1]), BF16),
            pltpu.VMEM((LANES, depth), BF16),
            pltpu.VMEM((HALO, wide), BF16),
            pltpu.VMEM(seg.shape, jnp.int32),
            pltpu.SemaphoreType.DMA((13,)),
            pltpu.SemaphoreType.DMA((13,)),
            pltpu.SemaphoreType.DMA((4,)),
        ],
        compiler_params=pltpu.CompilerParams(
            collective_id=0, has_side_effects=True, vmem_limit_bytes=VMEM_LIMIT
        ),
        name="gather_project",
    )(tokens, seg, w_z, w_x, w_bc, w_dt.T, w_out)


def scan_kernel(
    nt, heads,
    z, xbc, dt, halo, seg_before, seg, conv_x, conv_bc, gain, bias, rate, skip,
    g_out, ss_out,
    xs_s, b_s, c_s, segc, logs_s, dts_s, fresh_s, keep_s, y_s, local_s, decay_s,
    out0, out1, out2, in0, in1, in2, send, recv,
):
    t, x, c = here()
    after = at(lax.rem(t + 1, nt), x, c)
    before = at(lax.rem(t + nt - 1, nt), x, c)
    block, width = z.shape
    count = block // GROUP
    tiles = width // LANES
    head_dim = width // heads
    per = LANES // head_dim
    lane = lax.broadcasted_iota(jnp.int32, (1, LANES), 1)
    outs, ins = (out0, out1, out2), (in0, in1, in2)
    hops = [remote(outs[k], ins[k], send.at[k], recv.at[k], after) for k in range(3)]

    def scalars(ref):
        row = jnp.zeros((1, LANES), F32)
        for h in range(heads):
            row = jnp.where(lane == h, ref[h], row)
        return row

    def spread(cols, p):
        out = cols[:, p * per : p * per + 1]
        for q in range(1, per):
            out = jnp.where(lane >= q * head_dim, cols[:, p * per + q : p * per + q + 1], out)
        return jnp.broadcast_to(out, (cols.shape[0], LANES))

    greet((before,), 1)

    def columns(row):
        return jnp.transpose(jnp.broadcast_to(row.astype(F32), (LANES, LANES)))

    old = columns(seg_before[pl.ds(seg_before.shape[0] - 1, 1), :])
    old = jnp.where(t == 0, -1.0, old)
    segc[pl.ds(0, HALO), :] = old[LANES - HALO :, :]
    for i in range(block // LANES):
        segc[pl.ds(HALO + i * LANES, LANES), :] = columns(seg[pl.ds(i, 1), :])

    bias_row, rate_row = scalars(bias), scalars(rate)
    ones_low = (
        lax.broadcasted_iota(jnp.int32, (GROUP, GROUP), 0)
        >= lax.broadcasted_iota(jnp.int32, (GROUP, GROUP), 1)
    ).astype(F32)

    def first(g, carry):
        base = pl.multiple_of(g * GROUP, GROUP)
        mine = pl.ds(base, GROUP)
        back = pl.ds(pl.multiple_of(jnp.maximum(base - HALO, 0), HALO), HALO)
        sfull = segc[pl.ds(pl.multiple_of(base + 8, 8), GROUP + 8), :]
        scur = sfull[8:, :]
        same = [(pltpu.roll(sfull, 3 - k, 0)[8:, :] == scur).astype(F32) for k in range(3)]
        for j in range(tiles + 2):
            cols = pl.ds(j * LANES, LANES)
            prev = jnp.where(g == 0, halo[:, cols].astype(F32), xbc[back, cols].astype(F32))
            cur = xbc[mine, cols].astype(F32)
            full = jnp.concatenate([prev[8:, :], cur], axis=0)
            if j < tiles:
                taps = conv_x[:, cols]
            else:
                taps = conv_bc[:, pl.ds((j - tiles) * LANES, LANES)]
            total = pltpu.roll(full, 3, 0)[8:, :] * taps[0:1, :] * same[0]
            total = total + pltpu.roll(full, 2, 0)[8:, :] * taps[1:2, :] * same[1]
            total = total + pltpu.roll(full, 1, 0)[8:, :] * taps[2:3, :] * same[2]
            total = total + cur * taps[3:4, :]
            val = (total * (1.0 / (1.0 + jnp.exp(-total)))).astype(BF16)
            if j < tiles:
                xs_s[mine, cols] = val
            elif j == tiles:
                b_s[mine, :] = val
            else:
                c_s[mine, :] = val
        raw = dt[mine, :] + bias_row
        dts = jnp.maximum(raw, 0.0) + jnp.log1p(jnp.exp(-jnp.abs(raw)))
        logs = jnp.dot(
            ones_low, -dts * rate_row, preferred_element_type=F32, precision=lax.Precision.HIGHEST
        )
        dts_s[mine, :] = dts
        logs_s[mine, :] = logs
        final = logs[GROUP - 1 :, :]
        seg_last = scur[GROUP - 1 :, :]
        seg_in = sfull[7:8, :]
        tail = jnp.exp(final - logs) * (scur == seg_last).astype(F32) * dts
        keep = jnp.exp(final) * (seg_last == seg_in).astype(F32)
        scaled, kept = [], []
        for p in range(tiles):
            xs = xs_s[mine, pl.ds(p * LANES, LANES)].astype(F32)
            scaled.append((xs * spread(tail, p)).astype(BF16))
            kept.append(jnp.broadcast_to(spread(keep, p), (8, LANES)))
        keep_wide = jnp.concatenate(kept, axis=1)
        keep_s[pl.ds(pl.multiple_of(g * 8, 8), 8), :] = keep_wide
        fresh = lax.dot_general(
            b_s[mine, :], jnp.concatenate(scaled, axis=1), (((0,), (0,)), ((), ())),
            preferred_element_type=F32,
        )
        fresh_s[g] = fresh

        @pl.when(g == 0)
        def _():
            local_s[...] = fresh
            decay_s[...] = keep_wide

        @pl.when(g > 0)
        def _():
            local_s[...] = local_s[...] * keep_wide[0:1, :] + fresh
            decay_s[...] = decay_s[...] * keep_wide

        return carry

    lax.fori_loop(0, count, first, 0)
    out0[...] = local_s[...].astype(BF16)

    skip_rows = []
    for p in range(tiles):
        row = jnp.full((1, LANES), skip[p * per], F32)
        for q in range(1, per):
            row = jnp.where(lane >= q * head_dim, skip[p * per + q], row)
        skip_rows.append(row)
    below = lax.broadcasted_iota(jnp.int32, (LANES, LANES), 0) >= lax.broadcasted_iota(
        jnp.int32, (LANES, LANES), 1
    )

    def mix(g):
        base = pl.multiple_of(g * GROUP, GROUP)
        mine = pl.ds(base, GROUP)
        scur = segc[pl.ds(base + HALO, GROUP), :]
        srow = [seg[pl.ds(g * 2 + i, 1), :].astype(F32) for i in range(2)]
        scores = lax.dot_general(
            c_s[mine, :], b_s[mine, :], (((1,), (1,)), ((), ())), preferred_element_type=F32
        )
        lo, hi = slice(0, LANES), slice(LANES, GROUP)
        s00 = jnp.where(below & (scur[lo] == srow[0]), scores[lo, lo], 0.0)
        s10 = jnp.where(scur[hi] == srow[0], scores[hi, lo], 0.0)
        s11 = jnp.where(below & (scur[hi] == srow[1]), scores[hi, hi], 0.0)
        logs = logs_s[mine, :]
        lrow = jnp.transpose(logs)[0:8, :]
        drow = jnp.transpose(dts_s[mine, :])[0:8, :]
        for p in range(tiles):
            cols = pl.ds(p * LANES, LANES)
            xs = xs_s[mine, cols]
            total = None
            for q in range(per):
                h = p * per + q
                lc = logs[:, h : h + 1]
                lr, dr = lrow[h : h + 1, :], drow[h : h + 1, :]

                def piece(s, i, j):
                    return (s * jnp.exp(jnp.minimum(lc[i] - lr[:, j], 0.0)) * dr[:, j]).astype(BF16)

                top = jnp.concatenate([piece(s00, lo, lo), jnp.zeros((LANES, LANES), BF16)], axis=1)
                low = jnp.concatenate([piece(s10, hi, lo), piece(s11, hi, hi)], axis=1)
                part = (lane >= q * head_dim) & (lane < (q + 1) * head_dim)
                term = mm(
                    jnp.concatenate([top, low], axis=0), jnp.where(part, xs, jnp.zeros_like(xs))
                )
                total = term if total is None else total + term
            y_s[mine, cols] = total + skip_rows[p] * xs.astype(F32)

    mix(0)
    hops[0].start()
    mix(1)
    hops[0].wait_recv()
    decay = decay_s[0:1, :]
    out1[...] = (local_s[...] + decay * in0[...].astype(F32)).astype(BF16)
    hops[1].start()
    mix(2)
    hops[1].wait_recv()
    out2[...] = (local_s[...] + decay * in1[...].astype(F32)).astype(BF16)
    hops[2].start()
    mix(3)
    hops[2].wait_recv()
    local_s[...] = in2[...].astype(F32)
    eye = (
        lax.broadcasted_iota(jnp.int32, (LANES, LANES), 0)
        == lax.broadcasted_iota(jnp.int32, (LANES, LANES), 1)
    )

    def second(g, carry):
        base = pl.multiple_of(g * GROUP, GROUP)
        mine = pl.ds(base, GROUP)
        ssm = local_s[...]
        high = ssm.astype(BF16)
        low = (ssm - high.astype(F32)).astype(BF16)
        cm = c_s[mine, :]
        carried = mm(cm, high) + mm(cm, low)
        sfull = segc[pl.ds(pl.multiple_of(base + 8, 8), GROUP + 8), :]
        enter = jnp.exp(logs_s[mine, :]) * (sfull[8:, :] == sfull[7:8, :]).astype(F32)
        squares = jnp.zeros((GROUP, LANES), F32)
        for p in range(tiles):
            cols = pl.ds(p * LANES, LANES)
            zz = z[mine, cols].astype(F32)
            val = y_s[mine, cols] + carried[:, p * LANES : (p + 1) * LANES] * spread(enter, p)
            val = val * (zz * (1.0 / (1.0 + jnp.exp(-zz))))
            squares = squares + val * val
            g_out[mine, cols] = (val * gain[:, cols]).astype(BF16)
        sums = jnp.sum(squares, axis=1, keepdims=True)
        for i in range(GROUP // LANES):
            row = jnp.sum(jnp.where(eye, sums[i * LANES : (i + 1) * LANES, :], 0.0), axis=0, keepdims=True)
            ss_out[g * (GROUP // LANES) + i] = jnp.broadcast_to(row, (8, LANES))
        local_s[...] = ssm * keep_s[pl.ds(pl.multiple_of(g * 8, 8), 8), :][0:1, :] + fresh_s[g]
        return carry

    lax.fori_loop(0, count, second, 0)
    for hop in hops:
        hop.wait_send()


def scan(nt, z, xbc, dt, halo, seg_before, seg, conv_x, conv_bc, gain, bias, rate, skip):
    block, width = z.shape
    heads = rate.shape[0]
    count = block // GROUP
    state = LANES
    smem = whole(pltpu.SMEM)
    return pl.pallas_call(
        functools.partial(scan_kernel, nt, heads),
        out_shape=(
            jax.ShapeDtypeStruct((block, width), BF16),
            jax.ShapeDtypeStruct((block // LANES, 8, LANES), F32),
        ),
        in_specs=[whole()] * 9 + [smem] * 3,
        out_specs=(whole(), whole()),
        scratch_shapes=[
            pltpu.VMEM((block, width), BF16),
            pltpu.VMEM((block, state), BF16),
            pltpu.VMEM((block, state), BF16),
            pltpu.VMEM((block + HALO, LANES), F32),
            pltpu.VMEM((block, LANES), F32),
            pltpu.VMEM((block, LANES), F32),
            pltpu.VMEM((count, state, width), F32),
            pltpu.VMEM((count * 8, width), F32),
            pltpu.VMEM((block, width), F32),
            pltpu.VMEM((state, width), F32),
            pltpu.VMEM((8, width), F32),
        ]
        + [pltpu.VMEM((state, width), BF16)] * 6
        + [pltpu.SemaphoreType.DMA((3,)), pltpu.SemaphoreType.DMA((3,))],
        compiler_params=pltpu.CompilerParams(
            collective_id=1, has_side_effects=True, vmem_limit_bytes=VMEM_LIMIT
        ),
        name="scan_block",
    )(z, xbc, dt, halo, seg_before, seg, conv_x, conv_bc, gain, bias, rate, skip)


def scatter_kernel(
    nx, total_width, g_in, ss, wo, wo_mate, out,
    wo_v, g2, to_r, to_l, far_r, far_l, near_r, near_l, from_l, from_r, keep_r, keep_l, acc, ss_in,
    send, recv, local,
):
    t, x, c = here()
    n = 2 * nx
    w = x * 2 + c
    rows, cols = out.shape
    half = rows // 2
    width = g_in.shape[1]
    right = at(t, lax.rem(x + 1, nx), c)
    left = at(t, lax.rem(x + nx - 1, nx), c)
    mate = at(t, x, 1 - c)

    def rot(k):
        return lax.rem(x + k, nx)

    loads = [
        pltpu.make_async_copy(wo, wo_v.at[pl.ds(0, width)], local.at[0]),
        pltpu.make_async_copy(wo_mate, wo_v.at[pl.ds(width, width)], local.at[1]),
    ]
    order = (2, 1, nx - 1, 0)
    swaps = []
    for i, k in enumerate(order):
        xx = rot(k)
        to = pl.ds(pl.multiple_of(xx * rows, rows), rows)
        src = g_in.at[pl.ds(pl.multiple_of((xx * 2 + c) * rows, rows), rows)]
        loads.append(pltpu.make_async_copy(src, g2.at[to, pl.ds(0, width)], local.at[2 + i]))
        src = g_in.at[pl.ds(pl.multiple_of((xx * 2 + 1 - c) * rows, rows), rows)]
        swaps.append(remote(src, g2.at[to, pl.ds(width, width)], send.at[i], recv.at[i], mate))
    for load in loads:
        load.start()
    others = [
        {"tm": t, "weight": lax.rem(w + k, n)} for k in range(1, n)
    ]
    greet(others, n - 1)
    for swap in swaps:
        swap.start()
    sums = []
    for k in range(1, n):
        dest = lax.rem(w + k, n)
        sums.append(remote(ss.at[dest], ss_in.at[w], send.at[9 + k], recv.at[9 + k], others[k - 1]))
    for copy in sums:
        copy.start()
    r0 = remote(to_r, far_r, send.at[4], recv.at[4], right)
    l0 = remote(to_l, far_l, send.at[5], recv.at[5], left)
    r1 = remote(near_r.at[1], from_l.at[1], send.at[6], recv.at[6], right)
    l1 = remote(near_l.at[0], from_r.at[0], send.at[7], recv.at[7], left)
    r2 = remote(near_r.at[0], from_l.at[0], send.at[8], recv.at[8], right)
    l2 = remote(near_l.at[1], from_r.at[1], send.at[9], recv.at[9], left)
    for load in loads:
        load.wait()

    piece = 256
    spans = [pl.ds(i * piece, piece) for i in range(cols // piece)]

    def product(k, span):
        own = pl.ds(pl.multiple_of(rot(k) * rows, rows), rows)
        return mm(g2[own, :], wo_v[:, span])

    swaps[0].wait_recv()
    for span in spans:
        v = product(2, span).astype(BF16)
        to_r[:, span] = v[:half]
        to_l[:, span] = v[half:]
    r0.start()
    l0.start()
    swaps[1].wait_recv()
    for span in spans:
        v = product(1, span)
        keep_r[:, span] = v[:half]
        near_r[1, :, span] = v[half:].astype(BF16)
    r1.start()
    swaps[2].wait_recv()
    for span in spans:
        v = product(nx - 1, span)
        near_l[0, :, span] = v[:half].astype(BF16)
        keep_l[:, span] = v[half:]
    l1.start()
    swaps[3].wait_recv()
    for span in spans:
        acc[:, span] = product(0, span)
    r0.wait_recv()
    for span in spans:
        near_r[0, :, span] = (keep_r[:, span] + far_r[:, span].astype(F32)).astype(BF16)
    r2.start()
    l0.wait_recv()
    for span in spans:
        near_l[1, :, span] = (keep_l[:, span] + far_l[:, span].astype(F32)).astype(BF16)
    l2.start()
    for copy in sums:
        copy.wait_recv()
    ss_in[w] = ss[w]
    square = jnp.sum(ss_in[...], axis=0)[0:1, :]
    inverse = lax.rsqrt(square / total_width + EPS)
    eye = (
        lax.broadcasted_iota(jnp.int32, (rows, rows), 0)
        == lax.broadcasted_iota(jnp.int32, (rows, rows), 1)
    )
    scale = jnp.sum(jnp.where(eye, inverse, 0.0), axis=1, keepdims=True)
    r1.wait_recv()
    l1.wait_recv()
    for span in spans:
        acc[pl.ds(half, half), span] = acc[pl.ds(half, half), span] + from_l[1, :, span].astype(F32)
        acc[pl.ds(0, half), span] = acc[pl.ds(0, half), span] + from_r[0, :, span].astype(F32)
    r2.wait_recv()
    l2.wait_recv()
    for span in spans:
        v = acc[pl.ds(0, half), span] + from_l[0, :, span].astype(F32)
        out[pl.ds(0, half), span] = (v * scale[:half]).astype(BF16)
        v = acc[pl.ds(half, half), span] + from_r[1, :, span].astype(F32)
        out[pl.ds(half, half), span] = (v * scale[half:]).astype(BF16)
    for copy in swaps + sums + [r0, l0, r1, l1, r2, l2]:
        copy.wait_send()


def project_scatter(nx, g, ss, w_out, w_mate):
    block, width = g.shape
    n = 2 * nx
    rows = block // n
    half = rows // 2
    cols = w_out.shape[1]
    hbm = whole(pl.ANY)
    return pl.pallas_call(
        functools.partial(scatter_kernel, nx, width * n),
        out_shape=jax.ShapeDtypeStruct((rows, cols), BF16),
        in_specs=[hbm, whole(), hbm, hbm],
        out_specs=whole(),
        scratch_shapes=[
            pltpu.VMEM((2 * width, cols), BF16),
            pltpu.VMEM((nx * rows, 2 * width), BF16),
            pltpu.VMEM((half, cols), BF16),
            pltpu.VMEM((half, cols), BF16),
            pltpu.VMEM((half, cols), BF16),
            pltpu.VMEM((half, cols), BF16),
            pltpu.VMEM((2, half, cols), BF16),
            pltpu.VMEM((2, half, cols), BF16),
            pltpu.VMEM((2, half, cols), BF16),
            pltpu.VMEM((2, half, cols), BF16),
            pltpu.VMEM((half, cols), F32),
            pltpu.VMEM((half, cols), F32),
            pltpu.VMEM((rows, cols), F32),
            pltpu.VMEM((n, 8, LANES), F32),
            pltpu.SemaphoreType.DMA((9 + n,)),
            pltpu.SemaphoreType.DMA((9 + n,)),
            pltpu.SemaphoreType.DMA((6,)),
        ],
        compiler_params=pltpu.CompilerParams(
            collective_id=2, has_side_effects=True, vmem_limit_bytes=VMEM_LIMIT
        ),
        name="project_scatter",
    )(g, ss, w_out, w_mate)


def on_device(
    tokens, segments, w_z, w_x, w_dt, w_bc, conv_x, conv_bc, dt_bias, decay_rate, skip_d,
    norm_gain, w_out,
):
    nx = lax.axis_size("weight") // 2
    nt = lax.axis_size("tm")
    seg = segments.reshape(-1, LANES)
    gain = norm_gain.astype(F32).reshape(1, -1)
    z, xbc, dt, halo, seg_before, w_mate = gather_project(
        nx, nt, tokens, seg, w_z, w_x, w_bc, w_dt, w_out
    )
    g, ss = scan(
        nt, z, xbc, dt, halo, seg_before, seg, conv_x, conv_bc, gain, dt_bias, decay_rate, skip_d
    )
    return project_scatter(nx, g, ss, w_out, w_mate)


def solution(mesh):
    return jax.shard_map(
        on_device,
        mesh=mesh,
        in_specs=(
            P(("tm", "weight"), None),
            P("tm"),
            P(None, "weight"),
            P(None, "weight"),
            P(None, "weight"),
            P(),
            P(None, "weight"),
            P(),
            P("weight"),
            P("weight"),
            P("weight"),
            P("weight"),
            P("weight", None),
        ),
        out_specs=P(("tm", "weight"), None),
        check_vma=False,
    )
```

```python
import functools

import jax
import jax.numpy as jnp
from jax import lax
from jax.experimental import pallas as pl
from jax.experimental.pallas import tpu as pltpu
from jax.sharding import PartitionSpec as P

GROUP = 256
LANES = 128
HALO = 16
HOPS = 3
PIECE = 256
EPS = 1e-5
F32 = jnp.float32
BF16 = jnp.bfloat16
MESH = pl.DeviceIdType.MESH
VMEM_LIMIT = 56 * 1024 * 1024
COPIES = 64


def whole(space=pltpu.VMEM):
    return pl.BlockSpec(memory_space=space)


def mm(a, b):
    return jnp.dot(a, b, preferred_element_type=F32)


def silu(v):
    h = 0.5 * v
    return h + h * jnp.tanh(h)


def layer_kernel(
    nx, nt, heads,
    tok, seg, wz, wx, wbc, wdt, conv_x, conv_bc, gain, wo, bias, rate, skip,
    out,
    buf, wa_v, wz_v, wd_f, wo_v, z_s, xbc_s, dt_s, halo_s, seg_s,
    segc, mask_s, cv_s, cvh_s, xs_s, b_s, c_s, logs_s, dts_s, fresh_s, keep_s, y_s, ex_s, local_s, decay_s,
    ssm_s, kcum_s, hop_out, hop_in, enter_s, g_s, ss_s, ss_in,
    to_r, to_l, far_r, far_l, near_r, near_l, from_l, from_r, keep_r, keep_l, acc,
    send, recv, local,
):
    t = lax.axis_index("tm")
    w = lax.axis_index("weight")
    x, c = lax.div(w, 2), lax.rem(w, 2)
    n = 2 * nx
    rows, depth = tok.shape
    half, quarter = rows // 2, rows // 4
    width = wz.shape[1]
    block = rows * n
    tiles = width // LANES
    head_dim = width // heads
    per = LANES // head_dim
    lane = lax.broadcasted_iota(jnp.int32, (1, LANES), 1)

    def at(tt, xx, cc):
        return {"tm": tt, "weight": xx * 2 + cc}

    def rot(k):
        return lax.rem(x + (k + nx) % nx, nx)

    right, left, mate = at(t, rot(1), c), at(t, rot(-1), c), at(t, x, 1 - c)
    after = at(lax.rem(t + 1, nt), x, c)
    before = at(lax.rem(t + nt - 1, nt), x, c)
    copies = []

    def remote(src, dst, device):
        k = len(copies)
        copy = pltpu.make_async_remote_copy(
            src_ref=src, dst_ref=dst, send_sem=send.at[k], recv_sem=recv.at[k],
            device_id=device, device_id_type=MESH,
        )
        copies.append(copy)
        return copy

    def chunk(xx, start=0, size=rows):
        begin = (xx * 2 + c) * rows + start
        return buf.at[pl.ds(pl.multiple_of(begin, quarter), size)]

    def same_place(xx, start, size, device):
        return remote(chunk(xx, start, size), chunk(xx, start, size), device)

    own = pltpu.make_async_copy(tok, chunk(x), local.at[0])
    own.start()
    loads = [
        pltpu.make_async_copy(wx, wa_v.at[:, pl.ds(0, width)], local.at[1]),
        pltpu.make_async_copy(wbc, wa_v.at[:, pl.ds(width, wbc.shape[1])], local.at[2]),
        pltpu.make_async_copy(wz, wz_v, local.at[3]),
    ]
    for load in loads:
        load.start()
    load_wo = pltpu.make_async_copy(wo, wo_v.at[pl.ds(0, width)], local.at[4])
    load_wo.start()
    others = [{"tm": t, "weight": lax.rem(w + k, n)} for k in range(1, n)]
    barrier = pltpu.get_barrier_semaphore()
    for device in others + [before]:
        pl.semaphore_signal(barrier, inc=1, device_id=device, device_id_type=MESH)
    pl.semaphore_wait(barrier, n)

    xl, xr, xf = rot(-1), rot(1), rot(2)
    lo_half, hi_half = pl.ds(0, half), pl.ds(half, half)
    m0 = remote(tok, chunk(x), mate)
    a_r0 = remote(tok.at[lo_half], chunk(x, 0, half), right)
    a_l1 = remote(tok.at[hi_half], chunk(x, half, half), left)
    a_r1 = remote(tok.at[hi_half], chunk(x, half, half), right)
    a_l0 = remote(tok.at[lo_half], chunk(x, 0, half), left)
    to_seg = remote(seg, seg_s, after)
    for copy in (m0, a_r0, a_l1, a_r1, a_l0, to_seg):
        copy.start()
    to_wo = remote(wo, wo_v.at[pl.ds(width, width)], mate)
    to_wo.start()
    relay_r = [same_place(xl, q * quarter, quarter, right) for q in (0, 1)]
    relay_l = [same_place(xr, half + q * quarter, quarter, left) for q in (0, 1)]
    fwd_l0, fwd_l1 = same_place(xl, 0, half, mate), same_place(xl, half, half, mate)
    fwd_r1, fwd_r0 = same_place(xr, half, half, mate), same_place(xr, 0, half, mate)
    fwd_f = [
        [same_place(xf, q * quarter, quarter, mate), same_place(xf, half + q * quarter, quarter, mate)]
        for q in (0, 1)
    ]
    to_halo = remote(xbc_s.at[pl.ds(block - HALO, HALO)], halo_s, after)

    wd_f[...] = jnp.zeros_like(wd_f)
    wd_f[pl.ds(0, heads), :] = wdt[...].astype(F32)
    for i in range(depth // LANES):
        cols = pl.ds(i * LANES, LANES)
        part = jnp.concatenate([wd_f[:, cols], jnp.zeros((LANES - 8, LANES), F32)], axis=0)
        wa_v[cols, pl.ds(width + 2 * LANES, LANES)] = jnp.transpose(part).astype(BF16)

    def columns(row):
        return jnp.transpose(jnp.broadcast_to(row.astype(F32), (LANES, LANES)))

    def scalars(ref):
        row = jnp.zeros((1, LANES), F32)
        for h in range(heads):
            row = jnp.where(lane == h, ref[h], row)
        return row

    def spread(cols, p):
        value = cols[:, p * per : p * per + 1]
        for q in range(1, per):
            value = jnp.where(lane >= q * head_dim, cols[:, p * per + q : p * per + q + 1], value)
        return jnp.broadcast_to(value, (cols.shape[0], LANES))

    for i in range(block // LANES):
        segc[pl.ds(HALO + i * LANES, LANES), :] = columns(seg[pl.ds(i, 1), :])
    bias_row, rate_row = scalars(bias), scalars(rate)
    skip_rows = []
    for p in range(tiles):
        row = jnp.full((1, LANES), skip[p * per], F32)
        for q in range(1, per):
            row = jnp.where(lane >= q * head_dim, skip[p * per + q], row)
        skip_rows.append(row)

    to_seg.wait_recv()
    old = columns(seg_s[pl.ds(seg_s.shape[0] - 1, 1), :])
    old = jnp.where(t == 0, -1.0, old)
    segc[pl.ds(0, HALO), :] = old[LANES - HALO :, :]
    for k in range(3):
        for i in range(block // LANES):
            now = segc[pl.ds(HALO + i * LANES, LANES), :]
            then = segc[pl.ds(HALO + i * LANES - 3 + k, LANES), :]
            mask_s[k, pl.ds(i * LANES, LANES), :] = (now == then).astype(F32)

    def span(g, start=0, size=GROUP):
        return pl.ds(pl.multiple_of(g * GROUP + start, HALO), size)

    def project_xbc(g):
        mine = span(g)
        v = mm(buf[mine, :], wa_v[:, pl.ds(0, 256)]).astype(BF16)
        xbc_s[mine, pl.ds(0, 256)] = v
        v = mm(buf[mine, :], wa_v[:, pl.ds(256, 256)]).astype(BF16)
        xbc_s[mine, pl.ds(256, 256)] = v
        v = mm(buf[mine, :], wa_v[:, pl.ds(512, 256)]).astype(BF16)
        xbc_s[mine, pl.ds(512, 128)] = v[:, :128]
        dt_s[mine, :] = v[:, 128:].astype(F32)

    def halo_if_last(g):
        @pl.when(g == nx - 1)
        def _():
            to_halo.start()

    def project_z(g):
        mine = span(g)
        z_s[mine, pl.ds(0, 256)] = mm(buf[mine, :], wz_v[:, pl.ds(0, 256)]).astype(BF16)
        z_s[mine, pl.ds(256, 128)] = mm(buf[mine, :], wz_v[:, pl.ds(256, 128)]).astype(BF16)

    def taps_of(j):
        if j < tiles:
            return conv_x[:, pl.ds(j * LANES, LANES)]
        return conv_bc[:, pl.ds((j - tiles) * LANES, LANES)]

    def conv_store(j, where, val):
        if j < tiles:
            xs_s[where, pl.ds(j * LANES, LANES)] = val
        elif j == tiles:
            b_s[where, :] = val
        else:
            c_s[where, :] = val

    def conv_rows(j, source, g, start, size):
        taps = taps_of(j)
        mine = span(g, start, size)
        total = source[pl.ds(HALO - 3, size), :] * taps[0:1, :] * mask_s[0, mine, :]
        total = total + source[pl.ds(HALO - 2, size), :] * taps[1:2, :] * mask_s[1, mine, :]
        total = total + source[pl.ds(HALO - 1, size), :] * taps[2:3, :] * mask_s[2, mine, :]
        total = total + source[pl.ds(HALO, size), :] * taps[3:4, :]
        conv_store(j, mine, silu(total).astype(BF16))

    def conv_main(g):
        for j in range(tiles + 2):
            cv_s[j] = xbc_s[span(g), pl.ds(j * LANES, LANES)].astype(F32)
            conv_rows(j, cv_s.at[j], g, HALO, GROUP - HALO)

    def conv_head(g):
        for j in range(tiles + 2):
            cols = pl.ds(j * LANES, LANES)
            back = pl.ds(pl.multiple_of(jnp.maximum(g * GROUP - HALO, 0), HALO), HALO)

            @pl.when(g == 0)
            def _():
                cvh_s[j, pl.ds(0, HALO), :] = halo_s[:, cols].astype(F32)

            @pl.when(g > 0)
            def _():
                cvh_s[j, pl.ds(0, HALO), :] = xbc_s[back, cols].astype(F32)

            cvh_s[j, pl.ds(HALO, HALO), :] = xbc_s[span(g, 0, HALO), cols].astype(F32)
        for j in range(tiles + 2):
            conv_rows(j, cvh_s.at[j], g, 0, HALO)

    low_ones = (
        lax.broadcasted_iota(jnp.int32, (GROUP, GROUP), 0)
        >= lax.broadcasted_iota(jnp.int32, (GROUP, GROUP), 1)
    ).astype(F32).astype(BF16)

    def steps(g):
        mine = span(g)
        raw = dt_s[mine, :] + bias_row
        dts = jnp.maximum(raw, 0.0) + jnp.log1p(jnp.exp(-jnp.abs(raw)))
        rest = -dts * rate_row
        logs = jnp.zeros((GROUP, LANES), F32)
        for _ in range(3):
            part = rest.astype(BF16)
            rest = rest - part.astype(F32)
            logs = logs + mm(low_ones, part)
        dts_s[mine, :] = dts
        logs_s[mine, :] = logs

    def documents(g):
        base = g * GROUP
        cur = segc[pl.ds(pl.multiple_of(base + HALO, 8), GROUP), :]
        return cur, segc[pl.ds(pl.multiple_of(base + HALO - 8, 8), 8), :][7:8, :]

    def state(g):
        mine = span(g)
        logs, dts = logs_s[mine, :], dts_s[mine, :]
        cur, seg_in = documents(g)
        seg_last = cur[GROUP - 1 :, :]
        final = logs[GROUP - 1 :, :]
        tail = jnp.exp(final - logs) * (cur == seg_last).astype(F32) * dts
        keep = jnp.exp(final) * (seg_last == seg_in).astype(F32)
        scaled, kept = [], []
        for p in range(tiles):
            xs = xs_s[mine, pl.ds(p * LANES, LANES)].astype(F32)
            scaled.append((xs * spread(tail, p)).astype(BF16))
            kept.append(jnp.broadcast_to(spread(keep, p), (8, LANES)))
        keep_s[g] = jnp.concatenate(kept, axis=1)
        fresh_s[g] = lax.dot_general(
            b_s[mine, :], jnp.concatenate(scaled, axis=1), (((0,), (0,)), ((), ())),
            preferred_element_type=F32,
        )

    below = lax.broadcasted_iota(jnp.int32, (LANES, LANES), 0) >= lax.broadcasted_iota(
        jnp.int32, (LANES, LANES), 1
    )
    lo, hi = slice(0, LANES), slice(LANES, GROUP)

    def mix(g):
        mine = span(g)
        cur, seg_in = documents(g)
        srow = [seg[pl.ds(g * 2 + i, 1), :].astype(F32) for i in range(2)]
        scores = lax.dot_general(
            c_s[mine, :], b_s[mine, :], (((1,), (1,)), ((), ())), preferred_element_type=F32
        )
        s00 = jnp.where(below & (cur[lo] == srow[0]), scores[lo, lo], 0.0)
        s10 = jnp.where(cur[hi] == srow[0], scores[hi, lo], 0.0)
        s11 = jnp.where(below & (cur[hi] == srow[1]), scores[hi, hi], 0.0)
        logs = logs_s[mine, :]
        lrow = jnp.transpose(logs)[0:8, :]
        drow = jnp.transpose(dts_s[mine, :])[0:8, :]
        ssm = ssm_s[...]
        high = ssm.astype(BF16)
        low = (ssm - high.astype(F32)).astype(BF16)
        cm = c_s[mine, :]
        carried = mm(cm, high) + mm(cm, low)
        enter = jnp.exp(logs) * (cur == seg_in).astype(F32)
        for p in range(tiles):
            cols = pl.ds(p * LANES, LANES)
            xs = xs_s[mine, cols]
            total = None
            for q in range(per):
                h = p * per + q
                lc = logs[:, h : h + 1]
                lr, dr = lrow[h : h + 1, :], drow[h : h + 1, :]

                def piece(s, i, j):
                    return (s * jnp.exp(jnp.minimum(lc[i] - lr[:, j], 0.0)) * dr[:, j]).astype(BF16)

                top = jnp.concatenate([piece(s00, lo, lo), jnp.zeros((LANES, LANES), BF16)], axis=1)
                bot = jnp.concatenate([piece(s10, hi, lo), piece(s11, hi, hi)], axis=1)
                part = (lane >= q * head_dim) & (lane < (q + 1) * head_dim)
                term = mm(
                    jnp.concatenate([top, bot], axis=0), jnp.where(part, xs, jnp.zeros_like(xs))
                )
                total = term if total is None else total + term
            wide = spread(enter, p)
            gate = silu(z_s[mine, cols].astype(F32))
            inside = total + carried[:, p * LANES : (p + 1) * LANES] * wide
            y_s[mine, cols] = (inside + skip_rows[p] * xs.astype(F32)) * gate
            ex_s[mine, cols] = wide * kcum_s[0:1, cols] * gate
        kept = keep_s[g]
        ssm_s[...] = ssm * kept[0:1, :] + fresh_s[g]
        kcum_s[...] = kcum_s[...] * kept

    for load in loads:
        load.wait()
    own.wait()
    m0.wait_recv()
    project_xbc(x)
    halo_if_last(x)
    project_z(x)
    conv_main(x)
    steps(x)
    a_r0.wait_recv()
    a_l1.wait_recv()
    for copy in relay_r + relay_l + [fwd_l0, fwd_r1]:
        copy.start()
    a_r1.wait_recv()
    fwd_l1.start()
    a_l0.wait_recv()
    fwd_r0.start()
    fwd_l0.wait_recv()
    fwd_l1.wait_recv()
    project_xbc(xl)
    halo_if_last(xl)
    fwd_r1.wait_recv()
    fwd_r0.wait_recv()
    project_xbc(xr)
    halo_if_last(xr)
    relay_r[0].wait_recv()
    fwd_f[0][0].start()
    relay_l[0].wait_recv()
    fwd_f[0][1].start()
    conv_main(xl)
    steps(xl)
    conv_main(xr)
    steps(xr)

    def halo_wait(places):
        @pl.when(places)
        def _():
            to_halo.wait_recv()

    halo_wait((x == 0) | (x == nx - 1))

    conv_head(xr)
    relay_r[1].wait_recv()
    fwd_f[1][0].start()
    relay_l[1].wait_recv()
    fwd_f[1][1].start()
    state(xr)
    conv_head(x)
    state(x)
    project_z(xl)
    for pair in fwd_f:
        for copy in pair:
            copy.wait_recv()
    project_xbc(xf)
    halo_if_last(xf)
    conv_main(xf)
    steps(xf)
    halo_wait(x == 2)
    conv_head(xf)
    state(xf)
    halo_wait(x == 1)
    conv_head(xl)
    state(xl)

    hops = [
        [remote(hop_out.at[h, p], hop_in.at[h, p], after) for p in range(tiles)]
        for h in range(HOPS)
    ]
    for p in range(tiles):
        cols = pl.ds(p * LANES, LANES)
        total, decay = fresh_s[0, :, cols], keep_s[0, :, cols]
        for g in range(1, nx):
            total = total * keep_s[g, 0:1, cols] + fresh_s[g, :, cols]
            decay = decay * keep_s[g, :, cols]
        local_s[:, cols] = total
        decay_s[:, cols] = decay
        hop_out[0, p] = total.astype(BF16)
        hops[0][p].start()

    def hop_on(h):
        for p in range(tiles):
            cols = pl.ds(p * LANES, LANES)
            hops[h - 1][p].wait_recv()
            total = local_s[:, cols] + decay_s[0:1, cols] * hop_in[h - 1, p].astype(F32)
            hop_out[h, p] = total.astype(BF16)
            hops[h][p].start()

    ssm_s[...] = jnp.zeros_like(ssm_s)
    kcum_s[...] = jnp.ones_like(kcum_s)

    def mix_step(g, carry):
        mix(g)
        return carry

    project_z(xr)
    project_z(xf)
    lax.fori_loop(0, 1, mix_step, 0)
    hop_on(1)
    lax.fori_loop(1, 3, mix_step, 0)
    hop_on(2)
    lax.fori_loop(3, nx, mix_step, 0)
    load_wo.wait()
    to_wo.wait_recv()
    for p in range(tiles):
        hops[HOPS - 1][p].wait_recv()
        enter_s[:, pl.ds(p * LANES, LANES)] = hop_in[HOPS - 1, p]

    eye = (
        lax.broadcasted_iota(jnp.int32, (LANES, LANES), 0)
        == lax.broadcasted_iota(jnp.int32, (LANES, LANES), 1)
    )
    order = (2, 1, -1, 0)
    swaps = []
    for k in order:
        to = pl.ds(pl.multiple_of(rot(k) * rows, rows), rows)
        swaps.append(
            remote(g_s.at[1, to, pl.ds(0, width)], g_s.at[0, to, pl.ds(width, width)], mate)
        )

    def finish(k):
        g = rot(k)
        for i in range(2):
            mine = span(g, i * LANES, LANES)
            to = pl.ds(pl.multiple_of(g * rows, rows), rows)
            side = lax.rem(c + i, 2)
            carried = mm(c_s[mine, :], enter_s[...])
            squares = jnp.zeros((LANES, LANES), F32)
            for p in range(tiles):
                cols = pl.ds(p * LANES, LANES)
                val = y_s[mine, cols] + carried[:, p * LANES : (p + 1) * LANES] * ex_s[mine, cols]
                squares = squares + val * val
                g_s[side, to, cols] = (val * gain[:, cols]).astype(BF16)
            sums = jnp.sum(squares, axis=1, keepdims=True)
            row = jnp.sum(jnp.where(eye, sums, 0.0), axis=0, keepdims=True)
            ss_s[g * 2 + i] = jnp.broadcast_to(row, (8, LANES))

    spans = [pl.ds(i * PIECE, PIECE) for i in range(depth // PIECE)]
    first = (len(spans) + 1) // 2
    parts = [spans[:first], spans[first:]]
    part_cols = [pl.ds(0, first * PIECE), pl.ds(first * PIECE, depth - first * PIECE)]

    def product(k, cols):
        mine = pl.ds(pl.multiple_of(rot(k) * rows, rows), rows)
        return mm(g_s[0, mine, :], wo_v[:, cols])

    far = [
        (remote(to_r.at[:, cols], far_r.at[:, cols], right), remote(to_l.at[:, cols], far_l.at[:, cols], left))
        for cols in part_cols
    ]
    plain_r = remote(near_r.at[1], from_l.at[1], right)
    plain_l = remote(near_l.at[0], from_r.at[0], left)
    merged = [
        (
            remote(near_r.at[0, :, cols], from_l.at[0, :, cols], right),
            remote(near_l.at[1, :, cols], from_r.at[1, :, cols], left),
        )
        for cols in part_cols
    ]
    finish(2)
    swaps[0].start()
    finish(1)
    swaps[1].start()
    swaps[0].wait_recv()
    for part, pair in zip(parts, far):
        for cols in part:
            v = product(2, cols).astype(BF16)
            to_r[:, cols] = v[:half]
            to_l[:, cols] = v[half:]
        pair[0].start()
        pair[1].start()
    finish(-1)
    swaps[2].start()
    finish(0)
    swaps[3].start()
    sums = []
    for k in range(1, n):
        copy = remote(ss_s.at[lax.rem(w + k, n)], ss_in.at[w], others[k - 1])
        copy.start()
        sums.append(copy)
    swaps[1].wait_recv()
    for cols in spans:
        v = product(1, cols)
        keep_r[:, cols] = v[:half]
        near_r[1, :, cols] = v[half:].astype(BF16)
    plain_r.start()
    swaps[2].wait_recv()
    for cols in spans:
        v = product(-1, cols)
        near_l[0, :, cols] = v[:half].astype(BF16)
        keep_l[:, cols] = v[half:]
    plain_l.start()
    swaps[3].wait_recv()
    for cols in spans:
        acc[:, cols] = product(0, cols)
    for part, pair, ready in zip(parts, far, merged):
        pair[0].wait_recv()
        for cols in part:
            near_r[0, :, cols] = (keep_r[:, cols] + far_r[:, cols].astype(F32)).astype(BF16)
        ready[0].start()
        pair[1].wait_recv()
        for cols in part:
            near_l[1, :, cols] = (keep_l[:, cols] + far_l[:, cols].astype(F32)).astype(BF16)
        ready[1].start()
    for copy in sums:
        copy.wait_recv()
    ss_in[w] = ss_s[w]
    square = jnp.sum(ss_in[...], axis=0)[0:1, :]
    inverse = lax.rsqrt(square / (width * n) + EPS)
    scale = jnp.sum(jnp.where(eye, inverse, 0.0), axis=1, keepdims=True)
    plain_r.wait_recv()
    plain_l.wait_recv()
    for cols in spans:
        acc[hi_half, cols] = acc[hi_half, cols] + from_l[1, :, cols].astype(F32)
        acc[lo_half, cols] = acc[lo_half, cols] + from_r[0, :, cols].astype(F32)
    for part, pair in zip(parts, merged):
        pair[0].wait_recv()
        pair[1].wait_recv()
        for cols in part:
            v = acc[lo_half, cols] + from_l[0, :, cols].astype(F32)
            out[lo_half, cols] = (v * scale[:half]).astype(BF16)
            v = acc[hi_half, cols] + from_r[1, :, cols].astype(F32)
            out[hi_half, cols] = (v * scale[half:]).astype(BF16)
    assert len(copies) <= COPIES
    for copy in copies:
        if copy is not to_halo:
            copy.wait_send()
    to_halo.wait_send()


def on_device(
    tokens, segments, w_z, w_x, w_dt, w_bc, conv_x, conv_bc, dt_bias, decay_rate, skip_d,
    norm_gain, w_out,
):
    n = lax.axis_size("weight")
    nx, nt = n // 2, lax.axis_size("tm")
    seg = segments.reshape(-1, LANES)
    gain = norm_gain.astype(F32).reshape(1, -1)
    rows, depth = tokens.shape
    width, heads = w_z.shape[1], decay_rate.shape[0]
    block, half = rows * n, rows // 2
    tiles = width // LANES
    wide = width + w_bc.shape[1]
    count = block // GROUP
    hbm, vmem, smem = whole(pl.ANY), whole(), whole(pltpu.SMEM)
    V = pltpu.VMEM
    return pl.pallas_call(
        functools.partial(layer_kernel, nx, nt, heads),
        out_shape=jax.ShapeDtypeStruct((rows, depth), BF16),
        in_specs=[hbm, vmem, hbm, hbm, hbm, vmem, vmem, vmem, vmem, hbm, smem, smem, smem],
        out_specs=vmem,
        scratch_shapes=[
            V((block, depth), BF16),
            V((depth, wide + LANES), BF16),
            V((depth, width), BF16),
            V((8, depth), F32),
            V((2 * width, depth), BF16),
            V((block, width), BF16),
            V((block, wide), BF16),
            V((block, LANES), F32),
            V((HALO, wide), BF16),
            V(seg.shape, jnp.int32),
            V((block + HALO, LANES), F32),
            V((3, block, LANES), F32),
            V((tiles + 2, GROUP, LANES), F32),
            V((tiles + 2, 2 * HALO, LANES), F32),
            V((block, width), BF16),
            V((block, LANES), BF16),
            V((block, LANES), BF16),
            V((block, LANES), F32),
            V((block, LANES), F32),
            V((count, LANES, width), F32),
            V((count, 8, width), F32),
            V((block, width), F32),
            V((block, width), F32),
            V((LANES, width), F32),
            V((8, width), F32),
            V((LANES, width), F32),
            V((8, width), F32),
            V((HOPS, tiles, LANES, LANES), BF16),
            V((HOPS, tiles, LANES, LANES), BF16),
            V((LANES, width), BF16),
            V((2, nx * rows, 2 * width), BF16),
            V((n, 8, LANES), F32),
            V((n, 8, LANES), F32),
            V((half, depth), BF16),
            V((half, depth), BF16),
            V((half, depth), BF16),
            V((half, depth), BF16),
            V((2, half, depth), BF16),
            V((2, half, depth), BF16),
            V((2, half, depth), BF16),
            V((2, half, depth), BF16),
            V((half, depth), F32),
            V((half, depth), F32),
            V((rows, depth), F32),
            pltpu.SemaphoreType.DMA((COPIES,)),
            pltpu.SemaphoreType.DMA((COPIES,)),
            pltpu.SemaphoreType.DMA((5,)),
        ],
        compiler_params=pltpu.CompilerParams(
            collective_id=0, has_side_effects=True, vmem_limit_bytes=VMEM_LIMIT
        ),
        name="layer_block",
    )(
        tokens, seg, w_z, w_x, w_bc, w_dt.T, conv_x, conv_bc, gain, w_out,
        dt_bias, decay_rate, skip_d,
    )


def solution(mesh):
    return jax.shard_map(
        on_device,
        mesh=mesh,
        in_specs=(
            P(("tm", "weight"), None),
            P("tm"),
            P(None, "weight"),
            P(None, "weight"),
            P(None, "weight"),
            P(),
            P(None, "weight"),
            P(),
            P("weight"),
            P("weight"),
            P("weight"),
            P("weight"),
            P("weight", None),
        ),
        out_specs=P(("tm", "weight"), None),
        check_vma=False,
    )
```

```python
import functools

import jax
import jax.numpy as jnp
from jax import lax
from jax.experimental import pallas as pl
from jax.experimental.pallas import tpu as pltpu
from jax.sharding import PartitionSpec as P

GROUP = 256
LANES = 128
HALO = 16
HOPS = 3
PIECE = 256
EPS = 1e-5
F32 = jnp.float32
BF16 = jnp.bfloat16
MESH = pl.DeviceIdType.MESH
VMEM_LIMIT = 62 * 1024 * 1024
COPIES = 64


def whole(space=pltpu.VMEM):
    return pl.BlockSpec(memory_space=space)


def mm(a, b):
    return jnp.dot(a, b, preferred_element_type=F32)


def silu(v):
    h = 0.5 * v
    return h + h * jnp.tanh(h)


def layer_kernel(
    nx, nt, heads,
    tok, seg_h, wz, wx, wbc, wdt_h, conv_x_h, conv_bc_h, gain_h, wo, bias_h, rate_h, skip_h,
    out_h,
    seg, wdt, conv_x, conv_bc, gain_v, bias, rate, skip, out, buf, wa_v, wz_v, wd_f, wo_v, z_s, xbc_s, dt_s, halo_s, seg_s,
    segc, mask_s, cv_s, cvh_s, xs_s, b_s, c_s, logs_s, dts_s, fresh_s, keep_s, y_s, ex_s, local_s, decay_s,
    ssm_s, kcum_s, hop_out, hop_in, enter_s, g_s, ss_s, ss_in,
    to_r, to_l, far_r, far_l, near_r, near_l, from_l, from_r, keep_r, keep_l, acc,
    send, recv, local,
):
    t = lax.axis_index("tm")
    w = lax.axis_index("weight")
    x, c = lax.div(w, 2), lax.rem(w, 2)
    n = 2 * nx
    rows, depth = tok.shape
    half, quarter = rows // 2, rows // 4
    width = wz.shape[1]
    block = rows * n
    tiles = width // LANES
    head_dim = width // heads
    per = LANES // head_dim
    lane = lax.broadcasted_iota(jnp.int32, (1, LANES), 1)

    def at(tt, xx, cc):
        return {"tm": tt, "weight": xx * 2 + cc}

    def rot(k):
        return lax.rem(x + (k + nx) % nx, nx)

    right, left, mate = at(t, rot(1), c), at(t, rot(-1), c), at(t, x, 1 - c)
    after = at(lax.rem(t + 1, nt), x, c)
    before = at(lax.rem(t + nt - 1, nt), x, c)
    copies = []

    def remote(src, dst, device):
        k = len(copies)
        copy = pltpu.make_async_remote_copy(
            src_ref=src, dst_ref=dst, send_sem=send.at[k], recv_sem=recv.at[k],
            device_id=device, device_id_type=MESH,
        )
        copies.append(copy)
        return copy

    def chunk(xx, start=0, size=rows):
        begin = (xx * 2 + c) * rows + start
        return buf.at[pl.ds(pl.multiple_of(begin, quarter), size)]

    def same_place(xx, start, size, device):
        return remote(chunk(xx, start, size), chunk(xx, start, size), device)

    own = pltpu.make_async_copy(tok, chunk(x), local.at[0])
    own.start()
    smalls = [
        pltpu.make_async_copy(src, dst, local.at[5 + i])
        for i, (src, dst) in enumerate(
            [
                (seg_h, seg), (wdt_h, wdt), (conv_x_h, conv_x), (conv_bc_h, conv_bc),
                (gain_h, gain_v), (bias_h, bias), (rate_h, rate), (skip_h, skip),
            ]
        )
    ]
    for load in smalls:
        load.start()
    loads = [
        pltpu.make_async_copy(wx, wa_v.at[:, pl.ds(0, width)], local.at[1]),
        pltpu.make_async_copy(wbc, wa_v.at[:, pl.ds(width, wbc.shape[1])], local.at[2]),
        pltpu.make_async_copy(wz, wz_v, local.at[3]),
    ]
    for load in loads:
        load.start()
    load_wo = pltpu.make_async_copy(wo, wo_v.at[pl.ds(0, width)], local.at[4])
    load_wo.start()
    others = [{"tm": t, "weight": lax.rem(w + k, n)} for k in range(1, n)]
    barrier = pltpu.get_barrier_semaphore()
    for device in others:
        pl.semaphore_signal(barrier, inc=1, device_id=device, device_id_type=MESH)
    inner, outer = t > 0, t < nt - 1

    @pl.when(inner)
    def _():
        pl.semaphore_signal(barrier, inc=1, device_id=before, device_id_type=MESH)

    pl.semaphore_wait(barrier, jnp.where(outer, n, n - 1))

    def when_outer(act):
        pl.when(outer)(act)

    def when_inner(act):
        pl.when(inner)(act)

    xl, xr, xf = rot(-1), rot(1), rot(2)
    lo_half, hi_half = pl.ds(0, half), pl.ds(half, half)
    m0 = remote(tok, chunk(x), mate)
    a_r0 = remote(tok.at[lo_half], chunk(x, 0, half), right)
    a_l1 = remote(tok.at[hi_half], chunk(x, half, half), left)
    a_r1 = remote(tok.at[hi_half], chunk(x, half, half), right)
    a_l0 = remote(tok.at[lo_half], chunk(x, 0, half), left)
    to_seg = remote(seg_h, seg_s, after)
    for copy in (m0, a_r0, a_l1, a_r1, a_l0):
        copy.start()
    when_outer(to_seg.start)
    to_wo = remote(wo, wo_v.at[pl.ds(width, width)], mate)
    to_wo.start()
    relay_r = [same_place(xl, q * quarter, quarter, right) for q in (0, 1)]
    relay_l = [same_place(xr, half + q * quarter, quarter, left) for q in (0, 1)]
    fwd_l0, fwd_l1 = same_place(xl, 0, half, mate), same_place(xl, half, half, mate)
    fwd_r1, fwd_r0 = same_place(xr, half, half, mate), same_place(xr, 0, half, mate)
    fwd_f = [
        [same_place(xf, q * quarter, quarter, mate), same_place(xf, half + q * quarter, quarter, mate)]
        for q in (0, 1)
    ]
    to_halo = remote(xbc_s.at[pl.ds(block - HALO, HALO)], halo_s, after)

    for load in smalls:
        load.wait()
    gain = gain_v[...].astype(F32).reshape(1, width)

    @pl.when(t == 0)
    def _():
        seg_s[...] = jnp.zeros_like(seg_s)
        halo_s[...] = jnp.zeros_like(halo_s)
        hop_in[...] = jnp.zeros_like(hop_in)

    wd_f[...] = jnp.zeros_like(wd_f)
    wd_f[pl.ds(0, heads), :] = wdt[...].astype(F32)
    for i in range(depth // LANES):
        cols = pl.ds(i * LANES, LANES)
        part = jnp.concatenate([wd_f[:, cols], jnp.zeros((LANES - 8, LANES), F32)], axis=0)
        wa_v[cols, pl.ds(width + 2 * LANES, LANES)] = jnp.transpose(part).astype(BF16)

    def columns(row):
        return jnp.transpose(jnp.broadcast_to(row.astype(F32), (LANES, LANES)))

    def scalars(ref):
        row = jnp.zeros((1, LANES), F32)
        for h in range(heads):
            row = jnp.where(lane == h, ref[h], row)
        return row

    def spread(cols, p):
        value = cols[:, p * per : p * per + 1]
        for q in range(1, per):
            value = jnp.where(lane >= q * head_dim, cols[:, p * per + q : p * per + q + 1], value)
        return jnp.broadcast_to(value, (cols.shape[0], LANES))

    for i in range(block // LANES):
        segc[pl.ds(HALO + i * LANES, LANES), :] = columns(seg[pl.ds(i, 1), :])
    bias_row, rate_row = scalars(bias), scalars(rate)
    skip_rows = []
    for p in range(tiles):
        row = jnp.full((1, LANES), skip[p * per], F32)
        for q in range(1, per):
            row = jnp.where(lane >= q * head_dim, skip[p * per + q], row)
        skip_rows.append(row)

    when_inner(to_seg.wait_recv)
    old = columns(seg_s[pl.ds(seg_s.shape[0] - 1, 1), :])
    old = jnp.where(t == 0, -1.0, old)
    segc[pl.ds(0, HALO), :] = old[LANES - HALO :, :]
    for k in range(3):
        for i in range(block // LANES):
            now = segc[pl.ds(HALO + i * LANES, LANES), :]
            then = segc[pl.ds(HALO + i * LANES - 3 + k, LANES), :]
            mask_s[k, pl.ds(i * LANES, LANES), :] = (now == then).astype(F32)

    def span(g, start=0, size=GROUP):
        return pl.ds(pl.multiple_of(g * GROUP + start, HALO), size)

    def project_xbc(g):
        mine = span(g)
        v = mm(buf[mine, :], wa_v[:, pl.ds(0, 256)]).astype(BF16)
        xbc_s[mine, pl.ds(0, 256)] = v
        v = mm(buf[mine, :], wa_v[:, pl.ds(256, 256)]).astype(BF16)
        xbc_s[mine, pl.ds(256, 256)] = v
        v = mm(buf[mine, :], wa_v[:, pl.ds(512, 256)]).astype(BF16)
        xbc_s[mine, pl.ds(512, 128)] = v[:, :128]
        dt_s[mine, :] = v[:, 128:].astype(F32)

    def halo_if_last(g):
        @pl.when((g == nx - 1) & outer)
        def _():
            to_halo.start()

    def project_z(g):
        mine = span(g)
        z_s[mine, pl.ds(0, 256)] = mm(buf[mine, :], wz_v[:, pl.ds(0, 256)]).astype(BF16)
        z_s[mine, pl.ds(256, 128)] = mm(buf[mine, :], wz_v[:, pl.ds(256, 128)]).astype(BF16)

    def taps_of(j):
        if j < tiles:
            return conv_x[:, pl.ds(j * LANES, LANES)]
        return conv_bc[:, pl.ds((j - tiles) * LANES, LANES)]

    def conv_store(j, where, val):
        if j < tiles:
            xs_s[where, pl.ds(j * LANES, LANES)] = val
        elif j == tiles:
            b_s[where, :] = val
        else:
            c_s[where, :] = val

    def conv_rows(j, source, g, start, size):
        taps = taps_of(j)
        mine = span(g, start, size)
        total = source[pl.ds(HALO - 3, size), :] * taps[0:1, :] * mask_s[0, mine, :]
        total = total + source[pl.ds(HALO - 2, size), :] * taps[1:2, :] * mask_s[1, mine, :]
        total = total + source[pl.ds(HALO - 1, size), :] * taps[2:3, :] * mask_s[2, mine, :]
        total = total + source[pl.ds(HALO, size), :] * taps[3:4, :]
        conv_store(j, mine, silu(total).astype(BF16))

    def conv_main(g):
        for j in range(tiles + 2):
            cv_s[j] = xbc_s[span(g), pl.ds(j * LANES, LANES)].astype(F32)
            conv_rows(j, cv_s.at[j], g, HALO, GROUP - HALO)

    def conv_head(g):
        for j in range(tiles + 2):
            cols = pl.ds(j * LANES, LANES)
            back = pl.ds(pl.multiple_of(jnp.maximum(g * GROUP - HALO, 0), HALO), HALO)

            @pl.when(g == 0)
            def _():
                cvh_s[j, pl.ds(0, HALO), :] = halo_s[:, cols].astype(F32)

            @pl.when(g > 0)
            def _():
                cvh_s[j, pl.ds(0, HALO), :] = xbc_s[back, cols].astype(F32)

            cvh_s[j, pl.ds(HALO, HALO), :] = xbc_s[span(g, 0, HALO), cols].astype(F32)
        for j in range(tiles + 2):
            conv_rows(j, cvh_s.at[j], g, 0, HALO)

    low_ones = (
        lax.broadcasted_iota(jnp.int32, (GROUP, GROUP), 0)
        >= lax.broadcasted_iota(jnp.int32, (GROUP, GROUP), 1)
    ).astype(F32).astype(BF16)

    def steps(g):
        mine = span(g)
        raw = dt_s[mine, :] + bias_row
        dts = jnp.maximum(raw, 0.0) + jnp.log1p(jnp.exp(-jnp.abs(raw)))
        rest = -dts * rate_row
        logs = jnp.zeros((GROUP, LANES), F32)
        for _ in range(3):
            part = rest.astype(BF16)
            rest = rest - part.astype(F32)
            logs = logs + mm(low_ones, part)
        dts_s[mine, :] = dts
        logs_s[mine, :] = logs

    def documents(g):
        base = g * GROUP
        cur = segc[pl.ds(pl.multiple_of(base + HALO, 8), GROUP), :]
        return cur, segc[pl.ds(pl.multiple_of(base + HALO - 8, 8), 8), :][7:8, :]

    def state(g):
        mine = span(g)
        logs, dts = logs_s[mine, :], dts_s[mine, :]
        cur, seg_in = documents(g)
        seg_last = cur[GROUP - 1 :, :]
        final = logs[GROUP - 1 :, :]
        tail = jnp.exp(final - logs) * (cur == seg_last).astype(F32) * dts
        keep = jnp.exp(final) * (seg_last == seg_in).astype(F32)
        scaled, kept = [], []
        for p in range(tiles):
            xs = xs_s[mine, pl.ds(p * LANES, LANES)].astype(F32)
            scaled.append((xs * spread(tail, p)).astype(BF16))
            kept.append(jnp.broadcast_to(spread(keep, p), (8, LANES)))
        keep_s[g] = jnp.concatenate(kept, axis=1)
        fresh_s[g] = lax.dot_general(
            b_s[mine, :], jnp.concatenate(scaled, axis=1), (((0,), (0,)), ((), ())),
            preferred_element_type=F32,
        )

    below = lax.broadcasted_iota(jnp.int32, (LANES, LANES), 0) >= lax.broadcasted_iota(
        jnp.int32, (LANES, LANES), 1
    )
    lo, hi = slice(0, LANES), slice(LANES, GROUP)

    def mix(g):
        mine = span(g)
        cur, seg_in = documents(g)
        srow = [seg[pl.ds(g * 2 + i, 1), :].astype(F32) for i in range(2)]
        scores = lax.dot_general(
            c_s[mine, :], b_s[mine, :], (((1,), (1,)), ((), ())), preferred_element_type=F32
        )
        s00 = jnp.where(below & (cur[lo] == srow[0]), scores[lo, lo], 0.0)
        s10 = jnp.where(cur[hi] == srow[0], scores[hi, lo], 0.0)
        s11 = jnp.where(below & (cur[hi] == srow[1]), scores[hi, hi], 0.0)
        logs = logs_s[mine, :]
        lrow = jnp.transpose(logs)[0:8, :]
        drow = jnp.transpose(dts_s[mine, :])[0:8, :]
        ssm = ssm_s[...]
        high = ssm.astype(BF16)
        low = (ssm - high.astype(F32)).astype(BF16)
        cm = c_s[mine, :]
        carried = mm(cm, high) + mm(cm, low)
        enter = jnp.exp(logs) * (cur == seg_in).astype(F32)
        for p in range(tiles):
            cols = pl.ds(p * LANES, LANES)
            xs = xs_s[mine, cols]
            total = None
            for q in range(per):
                h = p * per + q
                lc = logs[:, h : h + 1]
                lr, dr = lrow[h : h + 1, :], drow[h : h + 1, :]

                def piece(s, i, j):
                    return (s * jnp.exp(jnp.minimum(lc[i] - lr[:, j], 0.0)) * dr[:, j]).astype(BF16)

                top = jnp.concatenate([piece(s00, lo, lo), jnp.zeros((LANES, LANES), BF16)], axis=1)
                bot = jnp.concatenate([piece(s10, hi, lo), piece(s11, hi, hi)], axis=1)
                part = (lane >= q * head_dim) & (lane < (q + 1) * head_dim)
                term = mm(
                    jnp.concatenate([top, bot], axis=0), jnp.where(part, xs, jnp.zeros_like(xs))
                )
                total = term if total is None else total + term
            wide = spread(enter, p)
            gate = silu(z_s[mine, cols].astype(F32))
            inside = total + carried[:, p * LANES : (p + 1) * LANES] * wide
            y_s[mine, cols] = (inside + skip_rows[p] * xs.astype(F32)) * gate
            ex_s[mine, cols] = wide * kcum_s[0:1, cols] * gate
        kept = keep_s[g]
        ssm_s[...] = ssm * kept[0:1, :] + fresh_s[g]
        kcum_s[...] = kcum_s[...] * kept

    for load in loads:
        load.wait()
    own.wait()
    m0.wait_recv()
    project_xbc(x)
    halo_if_last(x)
    project_z(x)
    conv_main(x)
    steps(x)
    a_r0.wait_recv()
    a_l1.wait_recv()
    for copy in relay_r + relay_l + [fwd_l0, fwd_r1]:
        copy.start()
    a_r1.wait_recv()
    fwd_l1.start()
    a_l0.wait_recv()
    fwd_r0.start()
    fwd_l0.wait_recv()
    fwd_l1.wait_recv()
    project_xbc(xl)
    halo_if_last(xl)
    fwd_r1.wait_recv()
    fwd_r0.wait_recv()
    project_xbc(xr)
    halo_if_last(xr)
    relay_r[0].wait_recv()
    fwd_f[0][0].start()
    relay_l[0].wait_recv()
    fwd_f[0][1].start()
    conv_main(xl)
    steps(xl)
    conv_main(xr)
    steps(xr)

    def halo_wait(places):
        @pl.when(places & inner)
        def _():
            to_halo.wait_recv()

    halo_wait((x == 0) | (x == nx - 1))

    conv_head(xr)
    relay_r[1].wait_recv()
    fwd_f[1][0].start()
    relay_l[1].wait_recv()
    fwd_f[1][1].start()
    state(xr)
    conv_head(x)
    state(x)
    project_z(xl)
    for pair in fwd_f:
        for copy in pair:
            copy.wait_recv()
    project_xbc(xf)
    halo_if_last(xf)
    conv_main(xf)
    steps(xf)
    halo_wait(x == 2)
    conv_head(xf)
    state(xf)
    halo_wait(x == 1)
    conv_head(xl)
    state(xl)

    hops = [
        [remote(hop_out.at[h, p], hop_in.at[h, p], after) for p in range(tiles)]
        for h in range(HOPS)
    ]
    for p in range(tiles):
        cols = pl.ds(p * LANES, LANES)
        total, decay = fresh_s[0, :, cols], keep_s[0, :, cols]
        for g in range(1, nx):
            total = total * keep_s[g, 0:1, cols] + fresh_s[g, :, cols]
            decay = decay * keep_s[g, :, cols]
        local_s[:, cols] = total
        decay_s[:, cols] = decay
        hop_out[0, p] = total.astype(BF16)
        when_outer(hops[0][p].start)

    def hop_on(h):
        for p in range(tiles):
            cols = pl.ds(p * LANES, LANES)
            when_inner(hops[h - 1][p].wait_recv)
            total = local_s[:, cols] + decay_s[0:1, cols] * hop_in[h - 1, p].astype(F32)
            hop_out[h, p] = total.astype(BF16)
            when_outer(hops[h][p].start)

    ssm_s[...] = jnp.zeros_like(ssm_s)
    kcum_s[...] = jnp.ones_like(kcum_s)

    def mix_step(g, carry):
        mix(g)
        return carry

    project_z(xr)
    project_z(xf)
    lax.fori_loop(0, 1, mix_step, 0)
    hop_on(1)
    lax.fori_loop(1, 2, mix_step, 0)
    hop_on(2)
    lax.fori_loop(2, nx, mix_step, 0)
    load_wo.wait()
    to_wo.wait_recv()
    for p in range(tiles):
        when_inner(hops[HOPS - 1][p].wait_recv)
        enter_s[:, pl.ds(p * LANES, LANES)] = hop_in[HOPS - 1, p]

    eye = (
        lax.broadcasted_iota(jnp.int32, (LANES, LANES), 0)
        == lax.broadcasted_iota(jnp.int32, (LANES, LANES), 1)
    )
    order = (2, 1, -1, 0)
    swaps = []
    for k in order:
        to = pl.ds(pl.multiple_of(rot(k) * rows, rows), rows)
        swaps.append(
            remote(g_s.at[1, to, pl.ds(0, width)], g_s.at[0, to, pl.ds(width, width)], mate)
        )

    def finish(k, swap):
        g = rot(k)
        for side in (1, 0):
            i = lax.rem(c + side, 2)
            mine = span(g, i * LANES, LANES)
            to = pl.ds(pl.multiple_of(g * rows, rows), rows)
            carried = mm(c_s[mine, :], enter_s[...])
            squares = jnp.zeros((LANES, LANES), F32)
            for p in range(tiles):
                cols = pl.ds(p * LANES, LANES)
                val = y_s[mine, cols] + carried[:, p * LANES : (p + 1) * LANES] * ex_s[mine, cols]
                squares = squares + val * val
                g_s[side, to, cols] = (val * gain[:, p * LANES : (p + 1) * LANES]).astype(BF16)
            sums = jnp.sum(squares, axis=1, keepdims=True)
            row = jnp.sum(jnp.where(eye, sums, 0.0), axis=0, keepdims=True)
            ss_s[g * 2 + i] = jnp.broadcast_to(row, (8, LANES))
            if side == 1:
                swap.start()

    spans = [pl.ds(i * PIECE, PIECE) for i in range(depth // PIECE)]
    first = (len(spans) + 1) // 2
    parts = [spans[:first], spans[first:]]
    part_cols = [pl.ds(0, first * PIECE), pl.ds(first * PIECE, depth - first * PIECE)]

    def product(k, cols):
        mine = pl.ds(pl.multiple_of(rot(k) * rows, rows), rows)
        return mm(g_s[0, mine, :], wo_v[:, cols])

    far = [
        (remote(to_r.at[:, cols], far_r.at[:, cols], right), remote(to_l.at[:, cols], far_l.at[:, cols], left))
        for cols in part_cols
    ]
    plain_r = remote(near_r.at[1], from_l.at[1], right)
    plain_l = remote(near_l.at[0], from_r.at[0], left)
    merged = [
        (
            remote(near_r.at[0, :, cols], from_l.at[0, :, cols], right),
            remote(near_l.at[1, :, cols], from_r.at[1, :, cols], left),
        )
        for cols in part_cols
    ]
    finish(2, swaps[0])
    finish(1, swaps[1])
    swaps[0].wait_recv()
    for part, pair in zip(parts, far):
        for cols in part:
            v = product(2, cols).astype(BF16)
            to_r[:, cols] = v[:half]
            to_l[:, cols] = v[half:]
        pair[0].start()
        pair[1].start()
    finish(-1, swaps[2])
    finish(0, swaps[3])
    sums = []
    for k in range(1, n):
        copy = remote(ss_s.at[lax.rem(w + k, n)], ss_in.at[w], others[k - 1])
        copy.start()
        sums.append(copy)
    swaps[1].wait_recv()
    for cols in spans:
        v = product(1, cols)
        keep_r[:, cols] = v[:half]
        near_r[1, :, cols] = v[half:].astype(BF16)
    plain_r.start()
    swaps[2].wait_recv()
    for cols in spans:
        v = product(-1, cols)
        near_l[0, :, cols] = v[:half].astype(BF16)
        keep_l[:, cols] = v[half:]
    plain_l.start()
    swaps[3].wait_recv()
    for cols in spans:
        acc[:, cols] = product(0, cols)
    for part, pair, ready in zip(parts, far, merged):
        pair[0].wait_recv()
        for cols in part:
            near_r[0, :, cols] = (keep_r[:, cols] + far_r[:, cols].astype(F32)).astype(BF16)
        ready[0].start()
        pair[1].wait_recv()
        for cols in part:
            near_l[1, :, cols] = (keep_l[:, cols] + far_l[:, cols].astype(F32)).astype(BF16)
        ready[1].start()
    for copy in sums:
        copy.wait_recv()
    ss_in[w] = ss_s[w]
    square = jnp.sum(ss_in[...], axis=0)[0:1, :]
    inverse = lax.rsqrt(square / (width * n) + EPS)
    scale = jnp.sum(jnp.where(eye, inverse, 0.0), axis=1, keepdims=True)
    plain_r.wait_recv()
    plain_l.wait_recv()
    for cols in spans:
        acc[hi_half, cols] = acc[hi_half, cols] + from_l[1, :, cols].astype(F32)
        acc[lo_half, cols] = acc[lo_half, cols] + from_r[0, :, cols].astype(F32)
    stores = [
        pltpu.make_async_copy(out.at[:, cols], out_h.at[:, cols], local.at[13 + i])
        for i, cols in enumerate(part_cols)
    ]
    for i, (part, pair) in enumerate(zip(parts, merged)):
        pair[0].wait_recv()
        pair[1].wait_recv()
        for cols in part:
            v = acc[lo_half, cols] + from_l[0, :, cols].astype(F32)
            out[lo_half, cols] = (v * scale[:half]).astype(BF16)
            v = acc[hi_half, cols] + from_r[1, :, cols].astype(F32)
            out[hi_half, cols] = (v * scale[half:]).astype(BF16)
        stores[i].start()
    assert len(copies) <= COPIES
    along = [to_seg, to_halo] + [hop for row in hops for hop in row]
    for copy in copies:
        if all(copy is not other for other in along):
            copy.wait_send()

    @pl.when(outer)
    def _():
        for copy in along:
            copy.wait_send()

    for store in stores:
        store.wait()


def on_device(
    tokens, segments, w_z, w_x, w_dt, w_bc, conv_x, conv_bc, dt_bias, decay_rate, skip_d,
    norm_gain, w_out,
):
    n = lax.axis_size("weight")
    nx, nt = n // 2, lax.axis_size("tm")
    seg = segments.reshape(-1, LANES)
    rows, depth = tokens.shape
    width, heads = w_z.shape[1], decay_rate.shape[0]
    block, half = rows * n, rows // 2
    tiles = width // LANES
    wide = width + w_bc.shape[1]
    count = block // GROUP
    hbm = whole(pl.ANY)
    V = pltpu.VMEM
    return pl.pallas_call(
        functools.partial(layer_kernel, nx, nt, heads),
        out_shape=jax.ShapeDtypeStruct((rows, depth), BF16),
        in_specs=[whole(pltpu.HBM)] * 13,
        out_specs=hbm,
        scratch_shapes=[
            V(seg.shape, jnp.int32),
            V((heads, depth), BF16),
            V(conv_x.shape, F32),
            V(conv_bc.shape, F32),
            V((width,), BF16),
            pltpu.SMEM((heads,), F32),
            pltpu.SMEM((heads,), F32),
            pltpu.SMEM((heads,), F32),
            V((rows, depth), BF16),
            V((block, depth), BF16),
            V((depth, wide + LANES), BF16),
            V((depth, width), BF16),
            V((8, depth), F32),
            V((2 * width, depth), BF16),
            V((block, width), BF16),
            V((block, wide), BF16),
            V((block, LANES), F32),
            V((HALO, wide), BF16),
            V(seg.shape, jnp.int32),
            V((block + HALO, LANES), F32),
            V((3, block, LANES), F32),
            V((tiles + 2, GROUP, LANES), F32),
            V((tiles + 2, 2 * HALO, LANES), F32),
            V((block, width), BF16),
            V((block, LANES), BF16),
            V((block, LANES), BF16),
            V((block, LANES), F32),
            V((block, LANES), F32),
            V((count, LANES, width), F32),
            V((count, 8, width), F32),
            V((block, width), F32),
            V((block, width), F32),
            V((LANES, width), F32),
            V((8, width), F32),
            V((LANES, width), F32),
            V((8, width), F32),
            V((HOPS, tiles, LANES, LANES), BF16),
            V((HOPS, tiles, LANES, LANES), BF16),
            V((LANES, width), BF16),
            V((2, nx * rows, 2 * width), BF16),
            V((n, 8, LANES), F32),
            V((n, 8, LANES), F32),
            V((half, depth), BF16),
            V((half, depth), BF16),
            V((half, depth), BF16),
            V((half, depth), BF16),
            V((2, half, depth), BF16),
            V((2, half, depth), BF16),
            V((2, half, depth), BF16),
            V((2, half, depth), BF16),
            V((half, depth), F32),
            V((half, depth), F32),
            V((rows, depth), F32),
            pltpu.SemaphoreType.DMA((COPIES,)),
            pltpu.SemaphoreType.DMA((COPIES,)),
            pltpu.SemaphoreType.DMA((15,)),
        ],
        compiler_params=pltpu.CompilerParams(
            collective_id=0, has_side_effects=True, vmem_limit_bytes=VMEM_LIMIT
        ),
        name="layer_block",
    )(
        tokens, seg, w_z, w_x, w_bc, w_dt.T, conv_x, conv_bc, norm_gain, w_out,
        dt_bias, decay_rate, skip_d,
    )


def solution(mesh):
    return jax.shard_map(
        on_device,
        mesh=mesh,
        in_specs=(
            P(("tm", "weight"), None),
            P("tm"),
            P(None, "weight"),
            P(None, "weight"),
            P(None, "weight"),
            P(),
            P(None, "weight"),
            P(),
            P("weight"),
            P("weight"),
            P("weight"),
            P("weight"),
            P("weight", None),
        ),
        out_specs=P(("tm", "weight"), None),
        check_vma=False,
    )
```

```python
import functools

import jax
import jax.numpy as jnp
from jax import lax
from jax.experimental import pallas as pl
from jax.experimental.pallas import tpu as pltpu
from jax.sharding import PartitionSpec as P

GROUP = 256
LANES = 128
HALO = 16
HOPS = 3
PARTS = 4
PIECE = 256
EPS = 1e-5
F32 = jnp.float32
BF16 = jnp.bfloat16
MESH = pl.DeviceIdType.MESH
VMEM_LIMIT = 62 * 1024 * 1024
COPIES = 80


def whole(space=pltpu.VMEM):
    return pl.BlockSpec(memory_space=space)


def mm(a, b):
    return jnp.dot(a, b, preferred_element_type=F32)


def silu(v):
    h = 0.5 * v
    return h + h * jnp.tanh(h)


def layer_kernel(
    nx, nt, heads,
    tok, seg_h, wz, wx, wbc, wdt_h, conv_x_h, conv_bc_h, gain_h, wo, bias_h, rate_h, skip_h,
    out_h,
    seg, wdt, conv_x, conv_bc, gain_v, bias, rate, skip, out, buf, wa_v, wz_v, wd_f, wo_v, z_s, xbc_s, dt_s, halo_s, seg_s,
    segc, mask_s, cv_s, cvh_s, xs_s, b_s, c_s, logs_s, dts_s, fresh_s, keep_s, y_s, ex_s, local_s, decay_s,
    ssm_s, kcum_s, hop_out, hop_in, enter_s, g_s, ss_s, ss_in,
    to_r, to_l, far_r, far_l, near_r, near_l, from_l, from_r, keep_r, keep_l, acc,
    send, recv, local,
):
    t = lax.axis_index("tm")
    w = lax.axis_index("weight")
    x, c = lax.div(w, 2), lax.rem(w, 2)
    n = 2 * nx
    rows, depth = tok.shape
    half, quarter = rows // 2, rows // 4
    width = wz.shape[1]
    block = rows * n
    tiles = width // LANES
    head_dim = width // heads
    per = LANES // head_dim
    lane = lax.broadcasted_iota(jnp.int32, (1, LANES), 1)

    def at(tt, xx, cc):
        return {"tm": tt, "weight": xx * 2 + cc}

    def rot(k):
        return lax.rem(x + (k + nx) % nx, nx)

    right, left, mate = at(t, rot(1), c), at(t, rot(-1), c), at(t, x, 1 - c)
    after = at(lax.rem(t + 1, nt), x, c)
    before = at(lax.rem(t + nt - 1, nt), x, c)
    copies = []

    def remote(src, dst, device):
        k = len(copies)
        copy = pltpu.make_async_remote_copy(
            src_ref=src, dst_ref=dst, send_sem=send.at[k], recv_sem=recv.at[k],
            device_id=device, device_id_type=MESH,
        )
        copies.append(copy)
        return copy

    def chunk(xx, start=0, size=rows):
        begin = (xx * 2 + c) * rows + start
        return buf.at[pl.ds(pl.multiple_of(begin, quarter), size)]

    def same_place(xx, start, size, device):
        return remote(chunk(xx, start, size), chunk(xx, start, size), device)

    own = pltpu.make_async_copy(tok, chunk(x), local.at[0])
    own.start()
    smalls = [
        pltpu.make_async_copy(src, dst, local.at[5 + i])
        for i, (src, dst) in enumerate(
            [
                (seg_h, seg), (wdt_h, wdt), (conv_x_h, conv_x), (conv_bc_h, conv_bc),
                (gain_h, gain_v), (bias_h, bias), (rate_h, rate), (skip_h, skip),
            ]
        )
    ]
    for load in smalls:
        load.start()
    loads = [
        pltpu.make_async_copy(wx, wa_v.at[:, pl.ds(0, width)], local.at[1]),
        pltpu.make_async_copy(wbc, wa_v.at[:, pl.ds(width, wbc.shape[1])], local.at[2]),
        pltpu.make_async_copy(wz, wz_v, local.at[3]),
    ]
    for load in loads:
        load.start()
    load_wo = pltpu.make_async_copy(wo, wo_v.at[pl.ds(0, width)], local.at[4])
    load_wo.start()
    others = [{"tm": t, "weight": lax.rem(w + k, n)} for k in range(1, n)]
    barrier = pltpu.get_barrier_semaphore()
    for device in others:
        pl.semaphore_signal(barrier, inc=1, device_id=device, device_id_type=MESH)
    inner, outer = t > 0, t < nt - 1

    @pl.when(inner)
    def _():
        pl.semaphore_signal(barrier, inc=1, device_id=before, device_id_type=MESH)

    pl.semaphore_wait(barrier, jnp.where(outer, n, n - 1))

    def when_outer(act):
        pl.when(outer)(act)

    def when_inner(act):
        pl.when(inner)(act)

    xl, xr, xf = rot(-1), rot(1), rot(2)
    lo_half, hi_half = pl.ds(0, half), pl.ds(half, half)
    m0 = remote(tok, chunk(x), mate)
    a_r0 = remote(tok.at[lo_half], chunk(x, 0, half), right)
    a_l1 = remote(tok.at[hi_half], chunk(x, half, half), left)
    a_r1 = remote(tok.at[hi_half], chunk(x, half, half), right)
    a_l0 = remote(tok.at[lo_half], chunk(x, 0, half), left)
    to_seg = remote(seg_h, seg_s, after)
    for copy in (m0, a_r0, a_l1, a_r1, a_l0):
        copy.start()
    when_outer(to_seg.start)
    to_wo = remote(wo, wo_v.at[pl.ds(width, width)], mate)
    to_wo.start()
    relay_r = [same_place(xl, q * quarter, quarter, right) for q in (0, 1)]
    relay_l = [same_place(xr, half + q * quarter, quarter, left) for q in (0, 1)]
    fwd_l0, fwd_l1 = same_place(xl, 0, half, mate), same_place(xl, half, half, mate)
    fwd_r1, fwd_r0 = same_place(xr, half, half, mate), same_place(xr, 0, half, mate)
    fwd_f = [
        [same_place(xf, q * quarter, quarter, mate), same_place(xf, half + q * quarter, quarter, mate)]
        for q in (0, 1)
    ]
    to_halo = remote(xbc_s.at[pl.ds(block - HALO, HALO)], halo_s, after)

    for load in smalls:
        load.wait()
    gain = gain_v[...].astype(F32).reshape(1, width)

    @pl.when(t == 0)
    def _():
        seg_s[...] = jnp.zeros_like(seg_s)
        halo_s[...] = jnp.zeros_like(halo_s)
        hop_in[...] = jnp.zeros_like(hop_in)

    wd_f[...] = jnp.zeros_like(wd_f)
    wd_f[pl.ds(0, heads), :] = wdt[...].astype(F32)
    for i in range(depth // LANES):
        cols = pl.ds(i * LANES, LANES)
        part = jnp.concatenate([wd_f[:, cols], jnp.zeros((LANES - 8, LANES), F32)], axis=0)
        wa_v[cols, pl.ds(width + 2 * LANES, LANES)] = jnp.transpose(part).astype(BF16)

    def columns(row):
        return jnp.transpose(jnp.broadcast_to(row.astype(F32), (LANES, LANES)))

    def scalars(ref):
        row = jnp.zeros((1, LANES), F32)
        for h in range(heads):
            row = jnp.where(lane == h, ref[h], row)
        return row

    def spread(cols, p):
        value = cols[:, p * per : p * per + 1]
        for q in range(1, per):
            value = jnp.where(lane >= q * head_dim, cols[:, p * per + q : p * per + q + 1], value)
        return jnp.broadcast_to(value, (cols.shape[0], LANES))

    for i in range(block // LANES):
        segc[pl.ds(HALO + i * LANES, LANES), :] = columns(seg[pl.ds(i, 1), :])
    bias_row, rate_row = scalars(bias), scalars(rate)
    skip_rows = []
    for p in range(tiles):
        row = jnp.full((1, LANES), skip[p * per], F32)
        for q in range(1, per):
            row = jnp.where(lane >= q * head_dim, skip[p * per + q], row)
        skip_rows.append(row)

    when_inner(to_seg.wait_recv)
    old = columns(seg_s[pl.ds(seg_s.shape[0] - 1, 1), :])
    old = jnp.where(t == 0, -1.0, old)
    segc[pl.ds(0, HALO), :] = old[LANES - HALO :, :]
    for k in range(3):
        for i in range(block // LANES):
            now = segc[pl.ds(HALO + i * LANES, LANES), :]
            then = segc[pl.ds(HALO + i * LANES - 3 + k, LANES), :]
            mask_s[k, pl.ds(i * LANES, LANES), :] = (now == then).astype(F32)

    def span(g, start=0, size=GROUP):
        return pl.ds(pl.multiple_of(g * GROUP + start, HALO), size)

    def project_xbc(g):
        mine = span(g)
        v = mm(buf[mine, :], wa_v[:, pl.ds(0, 256)]).astype(BF16)
        xbc_s[mine, pl.ds(0, 256)] = v
        v = mm(buf[mine, :], wa_v[:, pl.ds(256, 256)]).astype(BF16)
        xbc_s[mine, pl.ds(256, 256)] = v
        v = mm(buf[mine, :], wa_v[:, pl.ds(512, 256)]).astype(BF16)
        xbc_s[mine, pl.ds(512, 128)] = v[:, :128]
        dt_s[mine, :] = v[:, 128:].astype(F32)

    halves = [[(0, half), (rows, half)], [(half, half), (rows + half, half)]]
    quarters = [[(i * half + q * quarter, quarter) for i in range(4)] for q in range(2)]

    def some_rows(g, slices):
        mine = [span(g, *item) for item in slices]
        return mine, jnp.concatenate([buf[m, :] for m in mine], axis=0)

    def some_store(ref, mine, cols, v):
        size = v.shape[0] // len(mine)
        for i, m in enumerate(mine):
            ref[m, cols] = v[i * size : (i + 1) * size].astype(ref.dtype)

    def project_some(g, slices):
        mine, lhs = some_rows(g, slices)
        some_store(xbc_s, mine, pl.ds(0, 256), mm(lhs, wa_v[:, pl.ds(0, 256)]).astype(BF16))
        some_store(xbc_s, mine, pl.ds(256, 256), mm(lhs, wa_v[:, pl.ds(256, 256)]).astype(BF16))
        v = mm(lhs, wa_v[:, pl.ds(512, 256)]).astype(BF16)
        some_store(xbc_s, mine, pl.ds(512, 128), v[:, :128])
        some_store(dt_s, mine, pl.ds(0, 128), v[:, 128:])

    def project_z_some(g, slices):
        mine, lhs = some_rows(g, slices)
        some_store(z_s, mine, pl.ds(0, 256), mm(lhs, wz_v[:, pl.ds(0, 256)]).astype(BF16))
        some_store(z_s, mine, pl.ds(256, 128), mm(lhs, wz_v[:, pl.ds(256, 128)]).astype(BF16))

    def halo_if_last(g):
        @pl.when((g == nx - 1) & outer)
        def _():
            to_halo.start()

    def project_z(g):
        mine = span(g)
        z_s[mine, pl.ds(0, 256)] = mm(buf[mine, :], wz_v[:, pl.ds(0, 256)]).astype(BF16)
        z_s[mine, pl.ds(256, 128)] = mm(buf[mine, :], wz_v[:, pl.ds(256, 128)]).astype(BF16)

    def taps_of(j):
        if j < tiles:
            return conv_x[:, pl.ds(j * LANES, LANES)]
        return conv_bc[:, pl.ds((j - tiles) * LANES, LANES)]

    def conv_store(j, where, val):
        if j < tiles:
            xs_s[where, pl.ds(j * LANES, LANES)] = val
        elif j == tiles:
            b_s[where, :] = val
        else:
            c_s[where, :] = val

    def conv_rows(j, source, g, start, size):
        taps = taps_of(j)
        mine = span(g, start, size)
        total = source[pl.ds(HALO - 3, size), :] * taps[0:1, :] * mask_s[0, mine, :]
        total = total + source[pl.ds(HALO - 2, size), :] * taps[1:2, :] * mask_s[1, mine, :]
        total = total + source[pl.ds(HALO - 1, size), :] * taps[2:3, :] * mask_s[2, mine, :]
        total = total + source[pl.ds(HALO, size), :] * taps[3:4, :]
        conv_store(j, mine, silu(total).astype(BF16))

    def conv_main(g, tiles_of=tuple(range(width // LANES + 2))):
        for j in tiles_of:
            cv_s[j] = xbc_s[span(g), pl.ds(j * LANES, LANES)].astype(F32)
            conv_rows(j, cv_s.at[j], g, HALO, GROUP - HALO)

    def conv_head(g, tiles_of=tuple(range(width // LANES + 2))):
        for j in tiles_of:
            cols = pl.ds(j * LANES, LANES)
            back = pl.ds(pl.multiple_of(jnp.maximum(g * GROUP - HALO, 0), HALO), HALO)

            @pl.when(g == 0)
            def _():
                cvh_s[j, pl.ds(0, HALO), :] = halo_s[:, cols].astype(F32)

            @pl.when(g > 0)
            def _():
                cvh_s[j, pl.ds(0, HALO), :] = xbc_s[back, cols].astype(F32)

            cvh_s[j, pl.ds(HALO, HALO), :] = xbc_s[span(g, 0, HALO), cols].astype(F32)
        for j in tiles_of:
            conv_rows(j, cvh_s.at[j], g, 0, HALO)

    low_ones = (
        lax.broadcasted_iota(jnp.int32, (GROUP, GROUP), 0)
        >= lax.broadcasted_iota(jnp.int32, (GROUP, GROUP), 1)
    ).astype(F32).astype(BF16)

    def steps(g):
        mine = span(g)
        raw = dt_s[mine, :] + bias_row
        dts = jnp.maximum(raw, 0.0) + jnp.log1p(jnp.exp(-jnp.abs(raw)))
        rest = -dts * rate_row
        logs = jnp.zeros((GROUP, LANES), F32)
        for _ in range(3):
            part = rest.astype(BF16)
            rest = rest - part.astype(F32)
            logs = logs + mm(low_ones, part)
        dts_s[mine, :] = dts
        logs_s[mine, :] = logs

    def documents(g):
        base = g * GROUP
        cur = segc[pl.ds(pl.multiple_of(base + HALO, 8), GROUP), :]
        return cur, segc[pl.ds(pl.multiple_of(base + HALO - 8, 8), 8), :][7:8, :]

    def state(g):
        mine = span(g)
        logs, dts = logs_s[mine, :], dts_s[mine, :]
        cur, seg_in = documents(g)
        seg_last = cur[GROUP - 1 :, :]
        final = logs[GROUP - 1 :, :]
        tail = jnp.exp(final - logs) * (cur == seg_last).astype(F32) * dts
        keep = jnp.exp(final) * (seg_last == seg_in).astype(F32)
        scaled, kept = [], []
        for p in range(tiles):
            xs = xs_s[mine, pl.ds(p * LANES, LANES)].astype(F32)
            scaled.append((xs * spread(tail, p)).astype(BF16))
            kept.append(jnp.broadcast_to(spread(keep, p), (8, LANES)))
        keep_s[g] = jnp.concatenate(kept, axis=1)
        fresh_s[g] = lax.dot_general(
            b_s[mine, :], jnp.concatenate(scaled, axis=1), (((0,), (0,)), ((), ())),
            preferred_element_type=F32,
        )

    below = lax.broadcasted_iota(jnp.int32, (LANES, LANES), 0) >= lax.broadcasted_iota(
        jnp.int32, (LANES, LANES), 1
    )
    lo, hi = slice(0, LANES), slice(LANES, GROUP)

    def mix(g):
        mine = span(g)
        cur, seg_in = documents(g)
        srow = [seg[pl.ds(g * 2 + i, 1), :].astype(F32) for i in range(2)]
        scores = lax.dot_general(
            c_s[mine, :], b_s[mine, :], (((1,), (1,)), ((), ())), preferred_element_type=F32
        )
        s00 = jnp.where(below & (cur[lo] == srow[0]), scores[lo, lo], 0.0)
        s10 = jnp.where(cur[hi] == srow[0], scores[hi, lo], 0.0)
        s11 = jnp.where(below & (cur[hi] == srow[1]), scores[hi, hi], 0.0)
        logs = logs_s[mine, :]
        lrow = jnp.transpose(logs)[0:8, :]
        drow = jnp.transpose(dts_s[mine, :])[0:8, :]
        ssm = ssm_s[...]
        high = ssm.astype(BF16)
        low = (ssm - high.astype(F32)).astype(BF16)
        cm = c_s[mine, :]
        carried = mm(cm, high) + mm(cm, low)
        enter = jnp.exp(logs) * (cur == seg_in).astype(F32)
        for p in range(tiles):
            cols = pl.ds(p * LANES, LANES)
            xs = xs_s[mine, cols]
            total = None
            for q in range(per):
                h = p * per + q
                lc = logs[:, h : h + 1]
                lr, dr = lrow[h : h + 1, :], drow[h : h + 1, :]

                def piece(s, i, j):
                    return (s * jnp.exp(jnp.minimum(lc[i] - lr[:, j], 0.0)) * dr[:, j]).astype(BF16)

                top = jnp.concatenate([piece(s00, lo, lo), jnp.zeros((LANES, LANES), BF16)], axis=1)
                bot = jnp.concatenate([piece(s10, hi, lo), piece(s11, hi, hi)], axis=1)
                part = (lane >= q * head_dim) & (lane < (q + 1) * head_dim)
                term = mm(
                    jnp.concatenate([top, bot], axis=0), jnp.where(part, xs, jnp.zeros_like(xs))
                )
                total = term if total is None else total + term
            wide = spread(enter, p)
            gate = silu(z_s[mine, cols].astype(F32))
            inside = total + carried[:, p * LANES : (p + 1) * LANES] * wide
            y_s[mine, cols] = (inside + skip_rows[p] * xs.astype(F32)) * gate
            ex_s[mine, cols] = wide * kcum_s[0:1, cols] * gate
        kept = keep_s[g]
        ssm_s[...] = ssm * kept[0:1, :] + fresh_s[g]
        kcum_s[...] = kcum_s[...] * kept

    for load in loads:
        load.wait()
    own.wait()
    m0.wait_recv()
    project_xbc(x)
    halo_if_last(x)
    project_z(x)
    conv_main(x)
    steps(x)
    a_r0.wait_recv()
    a_l1.wait_recv()
    for copy in relay_r + relay_l + [fwd_l0, fwd_r1]:
        copy.start()
    fwd_l0.wait_recv()
    project_some(xl, halves[0])
    project_z_some(xl, halves[0])
    fwd_r1.wait_recv()
    project_some(xr, halves[1])
    halo_if_last(xr)
    project_z_some(xr, halves[1])
    a_r1.wait_recv()
    fwd_l1.start()
    a_l0.wait_recv()
    fwd_r0.start()
    fwd_l1.wait_recv()
    project_some(xl, halves[1])
    halo_if_last(xl)
    fwd_r0.wait_recv()
    project_some(xr, halves[0])
    project_z_some(xr, halves[0])
    relay_r[0].wait_recv()
    fwd_f[0][0].start()
    relay_l[0].wait_recv()
    fwd_f[0][1].start()
    conv_main(xl)
    steps(xl)
    conv_main(xr)
    steps(xr)

    def halo_wait(places):
        @pl.when(places & inner)
        def _():
            to_halo.wait_recv()

    halo_wait((x == 0) | (x == nx - 1))

    conv_head(xr)
    project_z_some(xl, halves[1])
    relay_r[1].wait_recv()
    fwd_f[1][0].start()
    relay_l[1].wait_recv()
    fwd_f[1][1].start()
    state(xr)
    conv_head(x)
    state(x)
    for slices, pair in zip(quarters, fwd_f):
        for copy in pair:
            copy.wait_recv()
        project_some(xf, slices)
    halo_if_last(xf)
    conv_main(xf, tuple(range(tiles + 1)))
    steps(xf)
    halo_wait(x == 2)
    conv_head(xf, tuple(range(tiles + 1)))
    state(xf)
    halo_wait(x == 1)
    conv_head(xl, tuple(range(tiles + 1)))
    state(xl)

    hops = [
        [remote(hop_out.at[h, p], hop_in.at[h, p], after) for p in range(tiles)]
        for h in range(HOPS)
    ]
    for p in range(tiles):
        cols = pl.ds(p * LANES, LANES)
        total, decay = fresh_s[0, :, cols], keep_s[0, :, cols]
        for g in range(1, nx):
            total = total * keep_s[g, 0:1, cols] + fresh_s[g, :, cols]
            decay = decay * keep_s[g, :, cols]
        local_s[:, cols] = total
        decay_s[:, cols] = decay
        hop_out[0, p] = total.astype(BF16)
        when_outer(hops[0][p].start)

    def hop_on(h):
        for p in range(tiles):
            cols = pl.ds(p * LANES, LANES)
            when_inner(hops[h - 1][p].wait_recv)
            total = local_s[:, cols] + decay_s[0:1, cols] * hop_in[h - 1, p].astype(F32)
            hop_out[h, p] = total.astype(BF16)
            when_outer(hops[h][p].start)

    ssm_s[...] = jnp.zeros_like(ssm_s)
    kcum_s[...] = jnp.ones_like(kcum_s)

    def mix_step(g, carry):
        mix(g)
        return carry

    conv_main(xf, (tiles + 1,))
    conv_head(xf, (tiles + 1,))
    conv_head(xl, (tiles + 1,))
    project_z(xf)
    lax.fori_loop(0, 1, mix_step, 0)
    hop_on(1)
    lax.fori_loop(1, 2, mix_step, 0)
    hop_on(2)
    lax.fori_loop(2, nx, mix_step, 0)
    load_wo.wait()
    to_wo.wait_recv()
    for p in range(tiles):
        when_inner(hops[HOPS - 1][p].wait_recv)
        enter_s[:, pl.ds(p * LANES, LANES)] = hop_in[HOPS - 1, p]

    eye = (
        lax.broadcasted_iota(jnp.int32, (LANES, LANES), 0)
        == lax.broadcasted_iota(jnp.int32, (LANES, LANES), 1)
    )
    order = (2, 1, -1, 0)
    swaps = []
    for k in order:
        to = pl.ds(pl.multiple_of(rot(k) * rows, rows), rows)
        swaps.append(
            remote(g_s.at[1, to, pl.ds(0, width)], g_s.at[0, to, pl.ds(width, width)], mate)
        )

    def finish(k, swap):
        g = rot(k)
        for side in (1, 0):
            i = lax.rem(c + side, 2)
            mine = span(g, i * LANES, LANES)
            to = pl.ds(pl.multiple_of(g * rows, rows), rows)
            carried = mm(c_s[mine, :], enter_s[...])
            squares = jnp.zeros((LANES, LANES), F32)
            for p in range(tiles):
                cols = pl.ds(p * LANES, LANES)
                val = y_s[mine, cols] + carried[:, p * LANES : (p + 1) * LANES] * ex_s[mine, cols]
                squares = squares + val * val
                g_s[side, to, cols] = (val * gain[:, p * LANES : (p + 1) * LANES]).astype(BF16)
            sums = jnp.sum(squares, axis=1, keepdims=True)
            row = jnp.sum(jnp.where(eye, sums, 0.0), axis=0, keepdims=True)
            ss_s[g * 2 + i] = jnp.broadcast_to(row, (8, LANES))
            if side == 1:
                swap.start()

    spans = [pl.ds(i * PIECE, PIECE) for i in range(depth // PIECE)]
    bounds = [len(spans) * i // PARTS for i in range(PARTS + 1)]
    parts = [spans[i:j] for i, j in zip(bounds, bounds[1:])]
    part_cols = [pl.ds(i * PIECE, (j - i) * PIECE) for i, j in zip(bounds, bounds[1:])]

    def product(k, cols):
        mine = pl.ds(pl.multiple_of(rot(k) * rows, rows), rows)
        return mm(g_s[0, mine, :], wo_v[:, cols])

    far = [
        (remote(to_r.at[:, cols], far_r.at[:, cols], right), remote(to_l.at[:, cols], far_l.at[:, cols], left))
        for cols in part_cols
    ]
    plain_r = remote(near_r.at[1], from_l.at[1], right)
    plain_l = remote(near_l.at[0], from_r.at[0], left)
    merged = [
        (
            remote(near_r.at[0, :, cols], from_l.at[0, :, cols], right),
            remote(near_l.at[1, :, cols], from_r.at[1, :, cols], left),
        )
        for cols in part_cols
    ]
    finish(2, swaps[0])
    finish(1, swaps[1])
    swaps[0].wait_recv()
    for part, pair in zip(parts, far):
        for cols in part:
            v = product(2, cols).astype(BF16)
            to_r[:, cols] = v[:half]
            to_l[:, cols] = v[half:]
        pair[0].start()
        pair[1].start()
    finish(-1, swaps[2])
    finish(0, swaps[3])
    sums = []
    for k in range(1, n):
        copy = remote(ss_s.at[lax.rem(w + k, n)], ss_in.at[w], others[k - 1])
        copy.start()
        sums.append(copy)
    swaps[1].wait_recv()
    for cols in spans:
        v = product(1, cols)
        keep_r[:, cols] = v[:half]
        near_r[1, :, cols] = v[half:].astype(BF16)
    plain_r.start()
    swaps[2].wait_recv()
    for cols in spans:
        v = product(-1, cols)
        near_l[0, :, cols] = v[:half].astype(BF16)
        keep_l[:, cols] = v[half:]
    plain_l.start()
    swaps[3].wait_recv()
    for cols in spans:
        acc[:, cols] = product(0, cols)
    for part, pair, ready in zip(parts, far, merged):
        pair[0].wait_recv()
        for cols in part:
            near_r[0, :, cols] = (keep_r[:, cols] + far_r[:, cols].astype(F32)).astype(BF16)
        ready[0].start()
        pair[1].wait_recv()
        for cols in part:
            near_l[1, :, cols] = (keep_l[:, cols] + far_l[:, cols].astype(F32)).astype(BF16)
        ready[1].start()
    for copy in sums:
        copy.wait_recv()
    ss_in[w] = ss_s[w]
    square = jnp.sum(ss_in[...], axis=0)[0:1, :]
    inverse = lax.rsqrt(square / (width * n) + EPS)
    scale = jnp.sum(jnp.where(eye, inverse, 0.0), axis=1, keepdims=True)
    plain_r.wait_recv()
    plain_l.wait_recv()
    for cols in spans:
        acc[hi_half, cols] = acc[hi_half, cols] + from_l[1, :, cols].astype(F32)
        acc[lo_half, cols] = acc[lo_half, cols] + from_r[0, :, cols].astype(F32)
    stores = [
        pltpu.make_async_copy(out.at[:, cols], out_h.at[:, cols], local.at[13 + i])
        for i, cols in enumerate(part_cols)
    ]
    for i, (part, pair) in enumerate(zip(parts, merged)):
        pair[0].wait_recv()
        pair[1].wait_recv()
        for cols in part:
            v = acc[lo_half, cols] + from_l[0, :, cols].astype(F32)
            out[lo_half, cols] = (v * scale[:half]).astype(BF16)
            v = acc[hi_half, cols] + from_r[1, :, cols].astype(F32)
            out[hi_half, cols] = (v * scale[half:]).astype(BF16)
        stores[i].start()
    assert len(copies) <= COPIES
    along = [to_seg, to_halo] + [hop for row in hops for hop in row]
    for copy in copies:
        if all(copy is not other for other in along):
            copy.wait_send()

    @pl.when(outer)
    def _():
        for copy in along:
            copy.wait_send()

    for store in stores:
        store.wait()


def on_device(
    tokens, segments, w_z, w_x, w_dt, w_bc, conv_x, conv_bc, dt_bias, decay_rate, skip_d,
    norm_gain, w_out,
):
    n = lax.axis_size("weight")
    nx, nt = n // 2, lax.axis_size("tm")
    seg = segments.reshape(-1, LANES)
    rows, depth = tokens.shape
    width, heads = w_z.shape[1], decay_rate.shape[0]
    block, half = rows * n, rows // 2
    tiles = width // LANES
    wide = width + w_bc.shape[1]
    count = block // GROUP
    hbm = whole(pl.ANY)
    V = pltpu.VMEM
    return pl.pallas_call(
        functools.partial(layer_kernel, nx, nt, heads),
        out_shape=jax.ShapeDtypeStruct((rows, depth), BF16),
        in_specs=[whole(pltpu.HBM)] * 13,
        out_specs=hbm,
        scratch_shapes=[
            V(seg.shape, jnp.int32),
            V((heads, depth), BF16),
            V(conv_x.shape, F32),
            V(conv_bc.shape, F32),
            V((width,), BF16),
            pltpu.SMEM((heads,), F32),
            pltpu.SMEM((heads,), F32),
            pltpu.SMEM((heads,), F32),
            V((rows, depth), BF16),
            V((block, depth), BF16),
            V((depth, wide + LANES), BF16),
            V((depth, width), BF16),
            V((8, depth), F32),
            V((2 * width, depth), BF16),
            V((block, width), BF16),
            V((block, wide), BF16),
            V((block, LANES), F32),
            V((HALO, wide), BF16),
            V(seg.shape, jnp.int32),
            V((block + HALO, LANES), F32),
            V((3, block, LANES), F32),
            V((tiles + 2, GROUP, LANES), F32),
            V((tiles + 2, 2 * HALO, LANES), F32),
            V((block, width), BF16),
            V((block, LANES), BF16),
            V((block, LANES), BF16),
            V((block, LANES), F32),
            V((block, LANES), F32),
            V((count, LANES, width), F32),
            V((count, 8, width), F32),
            V((block, width), F32),
            V((block, width), F32),
            V((LANES, width), F32),
            V((8, width), F32),
            V((LANES, width), F32),
            V((8, width), F32),
            V((HOPS, tiles, LANES, LANES), BF16),
            V((HOPS, tiles, LANES, LANES), BF16),
            V((LANES, width), BF16),
            V((2, nx * rows, 2 * width), BF16),
            V((n, 8, LANES), F32),
            V((n, 8, LANES), F32),
            V((half, depth), BF16),
            V((half, depth), BF16),
            V((half, depth), BF16),
            V((half, depth), BF16),
            V((2, half, depth), BF16),
            V((2, half, depth), BF16),
            V((2, half, depth), BF16),
            V((2, half, depth), BF16),
            V((half, depth), F32),
            V((half, depth), F32),
            V((rows, depth), F32),
            pltpu.SemaphoreType.DMA((COPIES,)),
            pltpu.SemaphoreType.DMA((COPIES,)),
            pltpu.SemaphoreType.DMA((13 + PARTS,)),
        ],
        compiler_params=pltpu.CompilerParams(
            collective_id=0, has_side_effects=True, vmem_limit_bytes=VMEM_LIMIT
        ),
        name="layer_block",
    )(
        tokens, seg, w_z, w_x, w_bc, w_dt.T, conv_x, conv_bc, norm_gain, w_out,
        dt_bias, decay_rate, skip_d,
    )


def solution(mesh):
    return jax.shard_map(
        on_device,
        mesh=mesh,
        in_specs=(
            P(("tm", "weight"), None),
            P("tm"),
            P(None, "weight"),
            P(None, "weight"),
            P(None, "weight"),
            P(),
            P(None, "weight"),
            P(),
            P("weight"),
            P("weight"),
            P("weight"),
            P("weight"),
            P("weight", None),
        ),
        out_specs=P(("tm", "weight"), None),
        check_vma=False,
    )
```

```python
import functools

import jax
import jax.numpy as jnp
from jax import lax
from jax.experimental import pallas as pl
from jax.experimental.pallas import tpu as pltpu
from jax.sharding import PartitionSpec as P

GROUP = 256
LANES = 128
HALO = 16
HOPS = 3
PARTS = 4
PIECE = 256
EPS = 1e-5
F32 = jnp.float32
BF16 = jnp.bfloat16
MESH = pl.DeviceIdType.MESH
VMEM_LIMIT = 62 * 1024 * 1024
COPIES = 80


def whole(space=pltpu.VMEM):
    return pl.BlockSpec(memory_space=space)


def mm(a, b):
    return jnp.dot(a, b, preferred_element_type=F32)


def silu(v):
    h = 0.5 * v
    return h + h * jnp.tanh(h)


def layer_kernel(
    nx, nt, heads,
    tok, seg_h, wz, wx, wbc, wdt_h, conv_x_h, conv_bc_h, gain_h, wo, bias_h, rate_h, skip_h,
    out_h,
    seg, wdt, conv_x, conv_bc, gain_v, bias, rate, skip, out, buf, wa_v, wz_v, wd_f, wo_v, z_s, xbc_s, dt_s, halo_s, seg_s,
    segc, mask_s, cv_s, cvh_s, xs_s, b_s, c_s, logs_s, dts_s, fresh_s, keep_s, y_s, ex_s, local_s, decay_s,
    ssm_s, kcum_s, hop_out, hop_in, enter_s, g_s, ss_s, ss_in,
    to_r, to_l, far_r, far_l, near_r, near_l, from_l, from_r, keep_r, keep_l, acc,
    send, recv, local, ready,
):
    t = lax.axis_index("tm")
    w = lax.axis_index("weight")
    x, c = lax.div(w, 2), lax.rem(w, 2)
    n = 2 * nx
    rows, depth = tok.shape
    half, quarter = rows // 2, rows // 4
    width = wz.shape[1]
    block = rows * n
    tiles = width // LANES
    head_dim = width // heads
    per = LANES // head_dim
    lane = lax.broadcasted_iota(jnp.int32, (1, LANES), 1)

    def at(tt, xx, cc):
        return {"tm": tt, "weight": xx * 2 + cc}

    def rot(k):
        return lax.rem(x + (k + nx) % nx, nx)

    right, left, mate = at(t, rot(1), c), at(t, rot(-1), c), at(t, x, 1 - c)
    after = at(lax.rem(t + 1, nt), x, c)
    before = at(lax.rem(t + nt - 1, nt), x, c)
    copies = []

    def remote(src, dst, device):
        k = len(copies)
        copy = pltpu.make_async_remote_copy(
            src_ref=src, dst_ref=dst, send_sem=send.at[k], recv_sem=recv.at[k],
            device_id=device, device_id_type=MESH,
        )
        copies.append(copy)
        return copy

    def chunk(xx, start=0, size=rows):
        begin = (xx * 2 + c) * rows + start
        return buf.at[pl.ds(pl.multiple_of(begin, quarter), size)]

    def same_place(xx, start, size, device):
        return remote(chunk(xx, start, size), chunk(xx, start, size), device)

    own = pltpu.make_async_copy(tok, chunk(x), local.at[0])
    own.start()
    smalls = [
        pltpu.make_async_copy(src, dst, local.at[5 + i])
        for i, (src, dst) in enumerate(
            [
                (seg_h, seg), (wdt_h, wdt), (conv_x_h, conv_x), (conv_bc_h, conv_bc),
                (gain_h, gain_v), (bias_h, bias), (rate_h, rate), (skip_h, skip),
            ]
        )
    ]
    for load in smalls:
        load.start()
    loads = [
        pltpu.make_async_copy(wx, wa_v.at[:, pl.ds(0, width)], local.at[1]),
        pltpu.make_async_copy(wbc, wa_v.at[:, pl.ds(width, wbc.shape[1])], local.at[2]),
        pltpu.make_async_copy(wz, wz_v, local.at[3]),
    ]
    for load in loads:
        load.start()
    load_wo = pltpu.make_async_copy(wo, wo_v.at[pl.ds(0, width)], local.at[4])
    load_wo.start()
    others = [{"tm": t, "weight": lax.rem(w + k, n)} for k in range(1, n)]
    barrier = pltpu.get_barrier_semaphore()
    for device in others:
        pl.semaphore_signal(barrier, inc=1, device_id=device, device_id_type=MESH)
    inner, outer = t > 0, t < nt - 1

    @pl.when(outer)
    def _():
        pl.semaphore_signal(barrier, inc=1, device_id=after, device_id_type=MESH)

    pl.semaphore_wait(barrier, jnp.where(inner, n, n - 1))

    def when_outer(act):
        pl.when(outer)(act)

    def when_inner(act):
        pl.when(inner)(act)

    xl, xr, xf = rot(-1), rot(1), rot(2)
    lo_half, hi_half = pl.ds(0, half), pl.ds(half, half)
    m0 = remote(tok, chunk(x), mate)
    a_r0 = remote(tok.at[lo_half], chunk(x, 0, half), right)
    a_l1 = remote(tok.at[hi_half], chunk(x, half, half), left)
    a_r1 = remote(tok.at[hi_half], chunk(x, half, half), right)
    a_l0 = remote(tok.at[lo_half], chunk(x, 0, half), left)
    to_seg = remote(seg_h, seg_s, after)
    for copy in (m0, a_r0, a_l1, a_r1, a_l0):
        copy.start()

    @pl.when(inner)
    def _():
        pl.semaphore_signal(ready, inc=1, device_id=before, device_id_type=MESH)

    to_wo = remote(wo, wo_v.at[pl.ds(width, width)], mate)
    to_wo.start()
    relay_r = [same_place(xl, q * quarter, quarter, right) for q in (0, 1)]
    relay_l = [same_place(xr, half + q * quarter, quarter, left) for q in (0, 1)]
    fwd_l0, fwd_l1 = same_place(xl, 0, half, mate), same_place(xl, half, half, mate)
    fwd_r1, fwd_r0 = same_place(xr, half, half, mate), same_place(xr, 0, half, mate)
    fwd_f = [
        [same_place(xf, q * quarter, quarter, mate), same_place(xf, half + q * quarter, quarter, mate)]
        for q in (0, 1)
    ]
    to_halo = remote(xbc_s.at[pl.ds(block - HALO, HALO)], halo_s, after)

    @pl.when(outer)
    def _():
        pl.semaphore_wait(ready, 1)
        to_seg.start()

    for load in smalls:
        load.wait()
    gain = gain_v[...].astype(F32).reshape(1, width)

    @pl.when(t == 0)
    def _():
        seg_s[...] = jnp.zeros_like(seg_s)
        halo_s[...] = jnp.zeros_like(halo_s)
        hop_in[...] = jnp.zeros_like(hop_in)

    wd_f[...] = jnp.zeros_like(wd_f)
    wd_f[pl.ds(0, heads), :] = wdt[...].astype(F32)
    for i in range(depth // LANES):
        cols = pl.ds(i * LANES, LANES)
        part = jnp.concatenate([wd_f[:, cols], jnp.zeros((LANES - 8, LANES), F32)], axis=0)
        wa_v[cols, pl.ds(width + 2 * LANES, LANES)] = jnp.transpose(part).astype(BF16)

    def columns(row):
        return jnp.transpose(jnp.broadcast_to(row.astype(F32), (LANES, LANES)))

    def scalars(ref):
        row = jnp.zeros((1, LANES), F32)
        for h in range(heads):
            row = jnp.where(lane == h, ref[h], row)
        return row

    def spread(cols, p):
        value = cols[:, p * per : p * per + 1]
        for q in range(1, per):
            value = jnp.where(lane >= q * head_dim, cols[:, p * per + q : p * per + q + 1], value)
        return jnp.broadcast_to(value, (cols.shape[0], LANES))

    for i in range(block // LANES):
        segc[pl.ds(HALO + i * LANES, LANES), :] = columns(seg[pl.ds(i, 1), :])
    bias_row, rate_row = scalars(bias), scalars(rate)
    skip_rows = []
    for p in range(tiles):
        row = jnp.full((1, LANES), skip[p * per], F32)
        for q in range(1, per):
            row = jnp.where(lane >= q * head_dim, skip[p * per + q], row)
        skip_rows.append(row)

    when_inner(to_seg.wait_recv)
    old = columns(seg_s[pl.ds(seg_s.shape[0] - 1, 1), :])
    old = jnp.where(t == 0, -1.0, old)
    segc[pl.ds(0, HALO), :] = old[LANES - HALO :, :]
    for k in range(3):
        for i in range(block // LANES):
            now = segc[pl.ds(HALO + i * LANES, LANES), :]
            then = segc[pl.ds(HALO + i * LANES - 3 + k, LANES), :]
            mask_s[k, pl.ds(i * LANES, LANES), :] = (now == then).astype(F32)

    def span(g, start=0, size=GROUP):
        return pl.ds(pl.multiple_of(g * GROUP + start, HALO), size)

    def project_xbc(g):
        mine = span(g)
        v = mm(buf[mine, :], wa_v[:, pl.ds(0, 256)]).astype(BF16)
        xbc_s[mine, pl.ds(0, 256)] = v
        v = mm(buf[mine, :], wa_v[:, pl.ds(256, 256)]).astype(BF16)
        xbc_s[mine, pl.ds(256, 256)] = v
        v = mm(buf[mine, :], wa_v[:, pl.ds(512, 256)]).astype(BF16)
        xbc_s[mine, pl.ds(512, 128)] = v[:, :128]
        dt_s[mine, :] = v[:, 128:].astype(F32)

    halves = [[(0, half), (rows, half)], [(half, half), (rows + half, half)]]
    quarters = [[(i * half + q * quarter, quarter) for i in range(4)] for q in range(2)]

    def some_rows(g, slices):
        mine = [span(g, *item) for item in slices]
        return mine, jnp.concatenate([buf[m, :] for m in mine], axis=0)

    def some_store(ref, mine, cols, v):
        size = v.shape[0] // len(mine)
        for i, m in enumerate(mine):
            ref[m, cols] = v[i * size : (i + 1) * size].astype(ref.dtype)

    def project_some(g, slices):
        mine, lhs = some_rows(g, slices)
        some_store(xbc_s, mine, pl.ds(0, 256), mm(lhs, wa_v[:, pl.ds(0, 256)]).astype(BF16))
        some_store(xbc_s, mine, pl.ds(256, 256), mm(lhs, wa_v[:, pl.ds(256, 256)]).astype(BF16))
        v = mm(lhs, wa_v[:, pl.ds(512, 256)]).astype(BF16)
        some_store(xbc_s, mine, pl.ds(512, 128), v[:, :128])
        some_store(dt_s, mine, pl.ds(0, 128), v[:, 128:])

    def project_z_some(g, slices):
        mine, lhs = some_rows(g, slices)
        some_store(z_s, mine, pl.ds(0, 256), mm(lhs, wz_v[:, pl.ds(0, 256)]).astype(BF16))
        some_store(z_s, mine, pl.ds(256, 128), mm(lhs, wz_v[:, pl.ds(256, 128)]).astype(BF16))

    def halo_if_last(g):
        @pl.when((g == nx - 1) & outer)
        def _():
            to_halo.start()

    def project_z(g):
        mine = span(g)
        z_s[mine, pl.ds(0, 256)] = mm(buf[mine, :], wz_v[:, pl.ds(0, 256)]).astype(BF16)
        z_s[mine, pl.ds(256, 128)] = mm(buf[mine, :], wz_v[:, pl.ds(256, 128)]).astype(BF16)

    def taps_of(j):
        if j < tiles:
            return conv_x[:, pl.ds(j * LANES, LANES)]
        return conv_bc[:, pl.ds((j - tiles) * LANES, LANES)]

    def conv_store(j, where, val):
        if j < tiles:
            xs_s[where, pl.ds(j * LANES, LANES)] = val
        elif j == tiles:
            b_s[where, :] = val
        else:
            c_s[where, :] = val

    def conv_rows(j, source, g, start, size):
        taps = taps_of(j)
        mine = span(g, start, size)
        total = source[pl.ds(HALO - 3, size), :] * taps[0:1, :] * mask_s[0, mine, :]
        total = total + source[pl.ds(HALO - 2, size), :] * taps[1:2, :] * mask_s[1, mine, :]
        total = total + source[pl.ds(HALO - 1, size), :] * taps[2:3, :] * mask_s[2, mine, :]
        total = total + source[pl.ds(HALO, size), :] * taps[3:4, :]
        conv_store(j, mine, silu(total).astype(BF16))

    def conv_main(g, tiles_of=tuple(range(width // LANES + 2))):
        for j in tiles_of:
            cv_s[j] = xbc_s[span(g), pl.ds(j * LANES, LANES)].astype(F32)
            conv_rows(j, cv_s.at[j], g, HALO, GROUP - HALO)

    def conv_head(g, tiles_of=tuple(range(width // LANES + 2))):
        for j in tiles_of:
            cols = pl.ds(j * LANES, LANES)
            back = pl.ds(pl.multiple_of(jnp.maximum(g * GROUP - HALO, 0), HALO), HALO)

            @pl.when(g == 0)
            def _():
                cvh_s[j, pl.ds(0, HALO), :] = halo_s[:, cols].astype(F32)

            @pl.when(g > 0)
            def _():
                cvh_s[j, pl.ds(0, HALO), :] = xbc_s[back, cols].astype(F32)

            cvh_s[j, pl.ds(HALO, HALO), :] = xbc_s[span(g, 0, HALO), cols].astype(F32)
        for j in tiles_of:
            conv_rows(j, cvh_s.at[j], g, 0, HALO)

    low_ones = (
        lax.broadcasted_iota(jnp.int32, (GROUP, GROUP), 0)
        >= lax.broadcasted_iota(jnp.int32, (GROUP, GROUP), 1)
    ).astype(F32).astype(BF16)

    def steps(g):
        mine = span(g)
        raw = dt_s[mine, :] + bias_row
        dts = jnp.maximum(raw, 0.0) + jnp.log1p(jnp.exp(-jnp.abs(raw)))
        rest = -dts * rate_row
        logs = jnp.zeros((GROUP, LANES), F32)
        for _ in range(3):
            part = rest.astype(BF16)
            rest = rest - part.astype(F32)
            logs = logs + mm(low_ones, part)
        dts_s[mine, :] = dts
        logs_s[mine, :] = logs

    def documents(g):
        base = g * GROUP
        cur = segc[pl.ds(pl.multiple_of(base + HALO, 8), GROUP), :]
        return cur, segc[pl.ds(pl.multiple_of(base + HALO - 8, 8), 8), :][7:8, :]

    def state(g):
        mine = span(g)
        logs, dts = logs_s[mine, :], dts_s[mine, :]
        cur, seg_in = documents(g)
        seg_last = cur[GROUP - 1 :, :]
        final = logs[GROUP - 1 :, :]
        tail = jnp.exp(final - logs) * (cur == seg_last).astype(F32) * dts
        keep = jnp.exp(final) * (seg_last == seg_in).astype(F32)
        scaled, kept = [], []
        for p in range(tiles):
            xs = xs_s[mine, pl.ds(p * LANES, LANES)].astype(F32)
            scaled.append((xs * spread(tail, p)).astype(BF16))
            kept.append(jnp.broadcast_to(spread(keep, p), (8, LANES)))
        keep_s[g] = jnp.concatenate(kept, axis=1)
        fresh_s[g] = lax.dot_general(
            b_s[mine, :], jnp.concatenate(scaled, axis=1), (((0,), (0,)), ((), ())),
            preferred_element_type=F32,
        )

    below = lax.broadcasted_iota(jnp.int32, (LANES, LANES), 0) >= lax.broadcasted_iota(
        jnp.int32, (LANES, LANES), 1
    )
    lo, hi = slice(0, LANES), slice(LANES, GROUP)

    def mix(g):
        mine = span(g)
        cur, seg_in = documents(g)
        srow = [seg[pl.ds(g * 2 + i, 1), :].astype(F32) for i in range(2)]
        scores = lax.dot_general(
            c_s[mine, :], b_s[mine, :], (((1,), (1,)), ((), ())), preferred_element_type=F32
        )
        s00 = jnp.where(below & (cur[lo] == srow[0]), scores[lo, lo], 0.0)
        s10 = jnp.where(cur[hi] == srow[0], scores[hi, lo], 0.0)
        s11 = jnp.where(below & (cur[hi] == srow[1]), scores[hi, hi], 0.0)
        logs = logs_s[mine, :]
        lrow = jnp.transpose(logs)[0:8, :]
        drow = jnp.transpose(dts_s[mine, :])[0:8, :]
        ssm = ssm_s[...]
        high = ssm.astype(BF16)
        low = (ssm - high.astype(F32)).astype(BF16)
        cm = c_s[mine, :]
        carried = mm(cm, high) + mm(cm, low)
        enter = jnp.exp(logs) * (cur == seg_in).astype(F32)
        for p in range(tiles):
            cols = pl.ds(p * LANES, LANES)
            xs = xs_s[mine, cols]
            total = None
            for q in range(per):
                h = p * per + q
                lc = logs[:, h : h + 1]
                lr, dr = lrow[h : h + 1, :], drow[h : h + 1, :]

                def piece(s, i, j):
                    return (s * jnp.exp(jnp.minimum(lc[i] - lr[:, j], 0.0)) * dr[:, j]).astype(BF16)

                top = jnp.concatenate([piece(s00, lo, lo), jnp.zeros((LANES, LANES), BF16)], axis=1)
                bot = jnp.concatenate([piece(s10, hi, lo), piece(s11, hi, hi)], axis=1)
                part = (lane >= q * head_dim) & (lane < (q + 1) * head_dim)
                term = mm(
                    jnp.concatenate([top, bot], axis=0), jnp.where(part, xs, jnp.zeros_like(xs))
                )
                total = term if total is None else total + term
            wide = spread(enter, p)
            gate = silu(z_s[mine, cols].astype(F32))
            inside = total + carried[:, p * LANES : (p + 1) * LANES] * wide
            y_s[mine, cols] = (inside + skip_rows[p] * xs.astype(F32)) * gate
            ex_s[mine, cols] = wide * kcum_s[0:1, cols] * gate
        kept = keep_s[g]
        ssm_s[...] = ssm * kept[0:1, :] + fresh_s[g]
        kcum_s[...] = kcum_s[...] * kept

    for load in loads:
        load.wait()
    own.wait()
    m0.wait_recv()
    project_xbc(x)
    halo_if_last(x)
    project_z(x)
    conv_main(x)
    steps(x)
    a_r0.wait_recv()
    a_l1.wait_recv()
    for copy in relay_r + relay_l + [fwd_l0, fwd_r1]:
        copy.start()
    fwd_l0.wait_recv()
    project_some(xl, halves[0])
    project_z_some(xl, halves[0])
    fwd_r1.wait_recv()
    project_some(xr, halves[1])
    halo_if_last(xr)
    project_z_some(xr, halves[1])
    a_r1.wait_recv()
    fwd_l1.start()
    a_l0.wait_recv()
    fwd_r0.start()
    fwd_l1.wait_recv()
    project_some(xl, halves[1])
    halo_if_last(xl)
    fwd_r0.wait_recv()
    project_some(xr, halves[0])
    project_z_some(xr, halves[0])
    relay_r[0].wait_recv()
    fwd_f[0][0].start()
    relay_l[0].wait_recv()
    fwd_f[0][1].start()
    conv_main(xl)
    steps(xl)
    conv_main(xr)
    steps(xr)

    def halo_wait(places):
        @pl.when(places & inner)
        def _():
            to_halo.wait_recv()

    halo_wait((x == 0) | (x == nx - 1))

    conv_head(xr)
    project_z_some(xl, halves[1])
    relay_r[1].wait_recv()
    fwd_f[1][0].start()
    relay_l[1].wait_recv()
    fwd_f[1][1].start()
    state(xr)
    conv_head(x)
    state(x)
    for slices, pair in zip(quarters, fwd_f):
        for copy in pair:
            copy.wait_recv()
        project_some(xf, slices)
    halo_if_last(xf)
    conv_main(xf, tuple(range(tiles + 1)))
    steps(xf)
    halo_wait(x == 2)
    conv_head(xf, tuple(range(tiles + 1)))
    state(xf)
    halo_wait(x == 1)
    conv_head(xl, tuple(range(tiles + 1)))
    state(xl)

    hops = [
        [remote(hop_out.at[h, p], hop_in.at[h, p], after) for p in range(tiles)]
        for h in range(HOPS)
    ]
    for p in range(tiles):
        cols = pl.ds(p * LANES, LANES)
        total, decay = fresh_s[0, :, cols], keep_s[0, :, cols]
        for g in range(1, nx):
            total = total * keep_s[g, 0:1, cols] + fresh_s[g, :, cols]
            decay = decay * keep_s[g, :, cols]
        local_s[:, cols] = total
        decay_s[:, cols] = decay
        hop_out[0, p] = total.astype(BF16)
        when_outer(hops[0][p].start)

    def hop_on(h):
        for p in range(tiles):
            cols = pl.ds(p * LANES, LANES)
            when_inner(hops[h - 1][p].wait_recv)
            total = local_s[:, cols] + decay_s[0:1, cols] * hop_in[h - 1, p].astype(F32)
            hop_out[h, p] = total.astype(BF16)
            when_outer(hops[h][p].start)

    ssm_s[...] = jnp.zeros_like(ssm_s)
    kcum_s[...] = jnp.ones_like(kcum_s)

    def mix_step(g, carry):
        mix(g)
        return carry

    conv_main(xf, (tiles + 1,))
    conv_head(xf, (tiles + 1,))
    conv_head(xl, (tiles + 1,))
    project_z(xf)
    lax.fori_loop(0, 1, mix_step, 0)
    hop_on(1)
    lax.fori_loop(1, 2, mix_step, 0)
    hop_on(2)
    lax.fori_loop(2, nx, mix_step, 0)
    load_wo.wait()
    to_wo.wait_recv()
    for p in range(tiles):
        when_inner(hops[HOPS - 1][p].wait_recv)
        enter_s[:, pl.ds(p * LANES, LANES)] = hop_in[HOPS - 1, p]

    eye = (
        lax.broadcasted_iota(jnp.int32, (LANES, LANES), 0)
        == lax.broadcasted_iota(jnp.int32, (LANES, LANES), 1)
    )
    order = (2, 1, -1, 0)
    swaps = []
    for k in order:
        to = pl.ds(pl.multiple_of(rot(k) * rows, rows), rows)
        swaps.append(
            remote(g_s.at[1, to, pl.ds(0, width)], g_s.at[0, to, pl.ds(width, width)], mate)
        )

    def finish(k, swap):
        g = rot(k)
        for side in (1, 0):
            i = lax.rem(c + side, 2)
            mine = span(g, i * LANES, LANES)
            to = pl.ds(pl.multiple_of(g * rows, rows), rows)
            carried = mm(c_s[mine, :], enter_s[...])
            squares = jnp.zeros((LANES, LANES), F32)
            for p in range(tiles):
                cols = pl.ds(p * LANES, LANES)
                val = y_s[mine, cols] + carried[:, p * LANES : (p + 1) * LANES] * ex_s[mine, cols]
                squares = squares + val * val
                g_s[side, to, cols] = (val * gain[:, p * LANES : (p + 1) * LANES]).astype(BF16)
            sums = jnp.sum(squares, axis=1, keepdims=True)
            row = jnp.sum(jnp.where(eye, sums, 0.0), axis=0, keepdims=True)
            ss_s[g * 2 + i] = jnp.broadcast_to(row, (8, LANES))
            if side == 1:
                swap.start()

    spans = [pl.ds(i * PIECE, PIECE) for i in range(depth // PIECE)]
    bounds = [len(spans) * i // PARTS for i in range(PARTS + 1)]
    parts = [spans[i:j] for i, j in zip(bounds, bounds[1:])]
    part_cols = [pl.ds(i * PIECE, (j - i) * PIECE) for i, j in zip(bounds, bounds[1:])]

    def product(k, cols):
        mine = pl.ds(pl.multiple_of(rot(k) * rows, rows), rows)
        return mm(g_s[0, mine, :], wo_v[:, cols])

    far = [
        (remote(to_r.at[:, cols], far_r.at[:, cols], right), remote(to_l.at[:, cols], far_l.at[:, cols], left))
        for cols in part_cols
    ]
    plain_r = remote(near_r.at[1], from_l.at[1], right)
    plain_l = remote(near_l.at[0], from_r.at[0], left)
    merged = [
        (
            remote(near_r.at[0, :, cols], from_l.at[0, :, cols], right),
            remote(near_l.at[1, :, cols], from_r.at[1, :, cols], left),
        )
        for cols in part_cols
    ]
    finish(2, swaps[0])
    finish(1, swaps[1])
    swaps[0].wait_recv()
    for part, pair in zip(parts, far):
        for cols in part:
            v = product(2, cols).astype(BF16)
            to_r[:, cols] = v[:half]
            to_l[:, cols] = v[half:]
        pair[0].start()
        pair[1].start()
    finish(-1, swaps[2])
    finish(0, swaps[3])
    sums = []
    for k in range(1, n):
        copy = remote(ss_s.at[lax.rem(w + k, n)], ss_in.at[w], others[k - 1])
        copy.start()
        sums.append(copy)
    swaps[1].wait_recv()
    for cols in spans:
        v = product(1, cols)
        keep_r[:, cols] = v[:half]
        near_r[1, :, cols] = v[half:].astype(BF16)
    plain_r.start()
    swaps[2].wait_recv()
    for cols in spans:
        v = product(-1, cols)
        near_l[0, :, cols] = v[:half].astype(BF16)
        keep_l[:, cols] = v[half:]
    plain_l.start()
    swaps[3].wait_recv()
    for cols in spans:
        acc[:, cols] = product(0, cols)
    for part, pair, ready in zip(parts, far, merged):
        pair[0].wait_recv()
        for cols in part:
            near_r[0, :, cols] = (keep_r[:, cols] + far_r[:, cols].astype(F32)).astype(BF16)
        ready[0].start()
        pair[1].wait_recv()
        for cols in part:
            near_l[1, :, cols] = (keep_l[:, cols] + far_l[:, cols].astype(F32)).astype(BF16)
        ready[1].start()
    for copy in sums:
        copy.wait_recv()
    ss_in[w] = ss_s[w]
    square = jnp.sum(ss_in[...], axis=0)[0:1, :]
    inverse = lax.rsqrt(square / (width * n) + EPS)
    scale = jnp.sum(jnp.where(eye, inverse, 0.0), axis=1, keepdims=True)
    plain_r.wait_recv()
    plain_l.wait_recv()
    for cols in spans:
        acc[hi_half, cols] = acc[hi_half, cols] + from_l[1, :, cols].astype(F32)
        acc[lo_half, cols] = acc[lo_half, cols] + from_r[0, :, cols].astype(F32)
    stores = [
        pltpu.make_async_copy(out.at[:, cols], out_h.at[:, cols], local.at[13 + i])
        for i, cols in enumerate(part_cols)
    ]
    for i, (part, pair) in enumerate(zip(parts, merged)):
        pair[0].wait_recv()
        pair[1].wait_recv()
        for cols in part:
            v = acc[lo_half, cols] + from_l[0, :, cols].astype(F32)
            out[lo_half, cols] = (v * scale[:half]).astype(BF16)
            v = acc[hi_half, cols] + from_r[1, :, cols].astype(F32)
            out[hi_half, cols] = (v * scale[half:]).astype(BF16)
        stores[i].start()
    assert len(copies) <= COPIES
    along = [to_seg, to_halo] + [hop for row in hops for hop in row]
    for copy in copies:
        if all(copy is not other for other in along):
            copy.wait_send()

    @pl.when(outer)
    def _():
        for copy in along:
            copy.wait_send()

    for store in stores:
        store.wait()


def on_device(
    tokens, segments, w_z, w_x, w_dt, w_bc, conv_x, conv_bc, dt_bias, decay_rate, skip_d,
    norm_gain, w_out,
):
    n = lax.axis_size("weight")
    nx, nt = n // 2, lax.axis_size("tm")
    seg = segments.reshape(-1, LANES)
    rows, depth = tokens.shape
    width, heads = w_z.shape[1], decay_rate.shape[0]
    block, half = rows * n, rows // 2
    tiles = width // LANES
    wide = width + w_bc.shape[1]
    count = block // GROUP
    hbm = whole(pl.ANY)
    V = pltpu.VMEM
    return pl.pallas_call(
        functools.partial(layer_kernel, nx, nt, heads),
        out_shape=jax.ShapeDtypeStruct((rows, depth), BF16),
        in_specs=[whole(pltpu.HBM)] * 13,
        out_specs=hbm,
        scratch_shapes=[
            V(seg.shape, jnp.int32),
            V((heads, depth), BF16),
            V(conv_x.shape, F32),
            V(conv_bc.shape, F32),
            V((width,), BF16),
            pltpu.SMEM((heads,), F32),
            pltpu.SMEM((heads,), F32),
            pltpu.SMEM((heads,), F32),
            V((rows, depth), BF16),
            V((block, depth), BF16),
            V((depth, wide + LANES), BF16),
            V((depth, width), BF16),
            V((8, depth), F32),
            V((2 * width, depth), BF16),
            V((block, width), BF16),
            V((block, wide), BF16),
            V((block, LANES), F32),
            V((HALO, wide), BF16),
            V(seg.shape, jnp.int32),
            V((block + HALO, LANES), F32),
            V((3, block, LANES), F32),
            V((tiles + 2, GROUP, LANES), F32),
            V((tiles + 2, 2 * HALO, LANES), F32),
            V((block, width), BF16),
            V((block, LANES), BF16),
            V((block, LANES), BF16),
            V((block, LANES), F32),
            V((block, LANES), F32),
            V((count, LANES, width), F32),
            V((count, 8, width), F32),
            V((block, width), F32),
            V((block, width), F32),
            V((LANES, width), F32),
            V((8, width), F32),
            V((LANES, width), F32),
            V((8, width), F32),
            V((HOPS, tiles, LANES, LANES), BF16),
            V((HOPS, tiles, LANES, LANES), BF16),
            V((LANES, width), BF16),
            V((2, nx * rows, 2 * width), BF16),
            V((n, 8, LANES), F32),
            V((n, 8, LANES), F32),
            V((half, depth), BF16),
            V((half, depth), BF16),
            V((half, depth), BF16),
            V((half, depth), BF16),
            V((2, half, depth), BF16),
            V((2, half, depth), BF16),
            V((2, half, depth), BF16),
            V((2, half, depth), BF16),
            V((half, depth), F32),
            V((half, depth), F32),
            V((rows, depth), F32),
            pltpu.SemaphoreType.DMA((COPIES,)),
            pltpu.SemaphoreType.DMA((COPIES,)),
            pltpu.SemaphoreType.DMA((13 + PARTS,)),
            pltpu.SemaphoreType.REGULAR,
        ],
        compiler_params=pltpu.CompilerParams(
            collective_id=0, has_side_effects=True, vmem_limit_bytes=VMEM_LIMIT
        ),
        name="layer_block",
    )(
        tokens, seg, w_z, w_x, w_bc, w_dt.T, conv_x, conv_bc, norm_gain, w_out,
        dt_bias, decay_rate, skip_d,
    )


def solution(mesh):
    return jax.shard_map(
        on_device,
        mesh=mesh,
        in_specs=(
            P(("tm", "weight"), None),
            P("tm"),
            P(None, "weight"),
            P(None, "weight"),
            P(None, "weight"),
            P(),
            P(None, "weight"),
            P(),
            P("weight"),
            P("weight"),
            P("weight"),
            P("weight"),
            P("weight", None),
        ),
        out_specs=P(("tm", "weight"), None),
        check_vma=False,
    )
```

```python
import functools

import jax
import jax.numpy as jnp
from jax import lax
from jax.experimental import pallas as pl
from jax.experimental.pallas import tpu as pltpu
from jax.sharding import PartitionSpec as P

GROUP = 256
LANES = 128
HALO = 16
HOPS = 3
PARTS = 4
PIECE = 256
EPS = 1e-5
F32 = jnp.float32
BF16 = jnp.bfloat16
MESH = pl.DeviceIdType.MESH
VMEM_LIMIT = 62 * 1024 * 1024
COPIES = 80


def whole(space=pltpu.VMEM):
    return pl.BlockSpec(memory_space=space)


def mm(a, b):
    return jnp.dot(a, b, preferred_element_type=F32)


def silu(v):
    h = 0.5 * v
    return h + h * jnp.tanh(h)


def layer_kernel(
    nx, nt, heads,
    tok, seg_h, wz, wx, wbc, wdt_h, conv_x_h, conv_bc_h, gain_h, wo, bias_h, rate_h, skip_h,
    out_h,
    seg, wdt, conv_x, conv_bc, gain_v, bias, rate, skip, out, buf, wa_v, wz_v, wd_f, wo_v, z_s, xbc_s, dt_s, halo_s, seg_s,
    segc, mask_s, cv_s, cvh_s, xs_s, b_s, c_s, logs_s, dts_s, fresh_s, keep_s, y_s, ex_s, local_s, decay_s,
    ssm_s, kcum_s, hop_out, hop_in, enter_s, g_s, ss_s, ss_in,
    to_r, to_l, far_r, far_l, near_r, near_l, from_l, from_r, keep_r, keep_l, acc,
    send, recv, local, ready,
):
    t = lax.axis_index("tm")
    w = lax.axis_index("weight")
    x, c = lax.div(w, 2), lax.rem(w, 2)
    n = 2 * nx
    rows, depth = tok.shape
    half, quarter = rows // 2, rows // 4
    width = wz.shape[1]
    block = rows * n
    tiles = width // LANES
    head_dim = width // heads
    per = LANES // head_dim
    lane = lax.broadcasted_iota(jnp.int32, (1, LANES), 1)

    def at(tt, xx, cc):
        return {"tm": tt, "weight": xx * 2 + cc}

    def rot(k):
        return lax.rem(x + (k + nx) % nx, nx)

    right, left, mate = at(t, rot(1), c), at(t, rot(-1), c), at(t, x, 1 - c)
    after = at(lax.rem(t + 1, nt), x, c)
    before = at(lax.rem(t + nt - 1, nt), x, c)
    copies = []

    def remote(src, dst, device):
        k = len(copies)
        copy = pltpu.make_async_remote_copy(
            src_ref=src, dst_ref=dst, send_sem=send.at[k], recv_sem=recv.at[k],
            device_id=device, device_id_type=MESH,
        )
        copies.append(copy)
        return copy

    def chunk(xx, start=0, size=rows):
        begin = (xx * 2 + c) * rows + start
        return buf.at[pl.ds(pl.multiple_of(begin, quarter), size)]

    def same_place(xx, start, size, device):
        return remote(chunk(xx, start, size), chunk(xx, start, size), device)

    own = pltpu.make_async_copy(tok, chunk(x), local.at[0])
    own.start()
    smalls = [
        pltpu.make_async_copy(src, dst, local.at[5 + i])
        for i, (src, dst) in enumerate(
            [
                (seg_h, seg), (wdt_h, wdt), (conv_x_h, conv_x), (conv_bc_h, conv_bc),
                (gain_h, gain_v), (bias_h, bias), (rate_h, rate), (skip_h, skip),
            ]
        )
    ]
    for load in smalls:
        load.start()
    loads = [
        pltpu.make_async_copy(wx, wa_v.at[:, pl.ds(0, width)], local.at[1]),
        pltpu.make_async_copy(wbc, wa_v.at[:, pl.ds(width, wbc.shape[1])], local.at[2]),
        pltpu.make_async_copy(wz, wz_v, local.at[3]),
    ]
    for load in loads:
        load.start()
    load_wo = pltpu.make_async_copy(wo, wo_v.at[pl.ds(0, width)], local.at[4])
    load_wo.start()
    others = [{"tm": t, "weight": lax.rem(w + k, n)} for k in range(1, n)]
    barrier = pltpu.get_barrier_semaphore()
    for device in others:
        pl.semaphore_signal(barrier, inc=1, device_id=device, device_id_type=MESH)
    inner, outer = t > 0, t < nt - 1

    @pl.when(outer)
    def _():
        pl.semaphore_signal(barrier, inc=1, device_id=after, device_id_type=MESH)

    pl.semaphore_wait(barrier, jnp.where(inner, n, n - 1))

    def when_outer(act):
        pl.when(outer)(act)

    def when_inner(act):
        pl.when(inner)(act)

    xl, xr, xf = rot(-1), rot(1), rot(2)
    lo_half, hi_half = pl.ds(0, half), pl.ds(half, half)
    m0 = remote(tok, chunk(x), mate)
    a_r0 = remote(tok.at[lo_half], chunk(x, 0, half), right)
    a_l1 = remote(tok.at[hi_half], chunk(x, half, half), left)
    a_r1 = remote(tok.at[hi_half], chunk(x, half, half), right)
    a_l0 = remote(tok.at[lo_half], chunk(x, 0, half), left)
    to_seg = remote(seg_h, seg_s, after)
    for copy in (m0, a_r0, a_l1, a_r1, a_l0):
        copy.start()

    @pl.when(inner)
    def _():
        pl.semaphore_signal(ready, inc=1, device_id=before, device_id_type=MESH)

    to_wo = remote(wo, wo_v.at[pl.ds(width, width)], mate)
    to_wo.start()
    relay_r = [same_place(xl, q * quarter, quarter, right) for q in (0, 1)]
    relay_l = [same_place(xr, half + q * quarter, quarter, left) for q in (0, 1)]
    fwd_l0, fwd_l1 = same_place(xl, 0, half, mate), same_place(xl, half, half, mate)
    fwd_r1, fwd_r0 = same_place(xr, half, half, mate), same_place(xr, 0, half, mate)
    fwd_f = [
        [same_place(xf, q * quarter, quarter, mate), same_place(xf, half + q * quarter, quarter, mate)]
        for q in (0, 1)
    ]
    to_halo = remote(xbc_s.at[pl.ds(block - HALO, HALO)], halo_s, after)

    @pl.when(outer)
    def _():
        pl.semaphore_wait(ready, 1)
        to_seg.start()

    for load in smalls:
        load.wait()
    gain = gain_v[...].astype(F32).reshape(1, width)

    @pl.when(t == 0)
    def _():
        seg_s[...] = jnp.zeros_like(seg_s)
        halo_s[...] = jnp.zeros_like(halo_s)
        hop_in[...] = jnp.zeros_like(hop_in)

    wd_f[...] = jnp.zeros_like(wd_f)
    wd_f[pl.ds(0, heads), :] = wdt[...].astype(F32)
    for i in range(depth // LANES):
        cols = pl.ds(i * LANES, LANES)
        part = jnp.concatenate([wd_f[:, cols], jnp.zeros((LANES - 8, LANES), F32)], axis=0)
        wa_v[cols, pl.ds(width + 2 * LANES, LANES)] = jnp.transpose(part).astype(BF16)

    def columns(row):
        return jnp.transpose(jnp.broadcast_to(row.astype(F32), (LANES, LANES)))

    def scalars(ref):
        row = jnp.zeros((1, LANES), F32)
        for h in range(heads):
            row = jnp.where(lane == h, ref[h], row)
        return row

    def spread(cols, p):
        value = cols[:, p * per : p * per + 1]
        for q in range(1, per):
            value = jnp.where(lane >= q * head_dim, cols[:, p * per + q : p * per + q + 1], value)
        return jnp.broadcast_to(value, (cols.shape[0], LANES))

    for i in range(block // LANES):
        segc[pl.ds(HALO + i * LANES, LANES), :] = columns(seg[pl.ds(i, 1), :])
    bias_row, rate_row = scalars(bias), scalars(rate)
    skip_rows = []
    for p in range(tiles):
        row = jnp.full((1, LANES), skip[p * per], F32)
        for q in range(1, per):
            row = jnp.where(lane >= q * head_dim, skip[p * per + q], row)
        skip_rows.append(row)

    when_inner(to_seg.wait_recv)
    old = columns(seg_s[pl.ds(seg_s.shape[0] - 1, 1), :])
    old = jnp.where(t == 0, -1.0, old)
    segc[pl.ds(0, HALO), :] = old[LANES - HALO :, :]
    for k in range(3):
        for i in range(block // LANES):
            now = segc[pl.ds(HALO + i * LANES, LANES), :]
            then = segc[pl.ds(HALO + i * LANES - 3 + k, LANES), :]
            mask_s[k, pl.ds(i * LANES, LANES), :] = (now == then).astype(F32)

    def span(g, start=0, size=GROUP):
        return pl.ds(pl.multiple_of(g * GROUP + start, HALO), size)

    def project_xbc(g):
        mine = span(g)
        v = mm(buf[mine, :], wa_v[:, pl.ds(0, 256)]).astype(BF16)
        xbc_s[mine, pl.ds(0, 256)] = v
        v = mm(buf[mine, :], wa_v[:, pl.ds(256, 256)]).astype(BF16)
        xbc_s[mine, pl.ds(256, 256)] = v
        v = mm(buf[mine, :], wa_v[:, pl.ds(512, 256)]).astype(BF16)
        xbc_s[mine, pl.ds(512, 128)] = v[:, :128]
        dt_s[mine, :] = v[:, 128:].astype(F32)

    halves = [[(0, half), (rows, half)], [(half, half), (rows + half, half)]]
    quarters = [[(i * half + q * quarter, quarter) for i in range(4)] for q in range(2)]

    def some_rows(g, slices):
        mine = [span(g, *item) for item in slices]
        return mine, jnp.concatenate([buf[m, :] for m in mine], axis=0)

    def some_store(ref, mine, cols, v):
        size = v.shape[0] // len(mine)
        for i, m in enumerate(mine):
            ref[m, cols] = v[i * size : (i + 1) * size].astype(ref.dtype)

    def project_some(g, slices):
        mine, lhs = some_rows(g, slices)
        some_store(xbc_s, mine, pl.ds(0, 256), mm(lhs, wa_v[:, pl.ds(0, 256)]).astype(BF16))
        some_store(xbc_s, mine, pl.ds(256, 256), mm(lhs, wa_v[:, pl.ds(256, 256)]).astype(BF16))
        v = mm(lhs, wa_v[:, pl.ds(512, 256)]).astype(BF16)
        some_store(xbc_s, mine, pl.ds(512, 128), v[:, :128])
        some_store(dt_s, mine, pl.ds(0, 128), v[:, 128:])

    def project_z_some(g, slices):
        mine, lhs = some_rows(g, slices)
        some_store(z_s, mine, pl.ds(0, 256), mm(lhs, wz_v[:, pl.ds(0, 256)]).astype(BF16))
        some_store(z_s, mine, pl.ds(256, 128), mm(lhs, wz_v[:, pl.ds(256, 128)]).astype(BF16))

    def halo_if_last(g):
        @pl.when((g == nx - 1) & outer)
        def _():
            to_halo.start()

    def project_z(g):
        mine = span(g)
        z_s[mine, pl.ds(0, 256)] = mm(buf[mine, :], wz_v[:, pl.ds(0, 256)]).astype(BF16)
        z_s[mine, pl.ds(256, 128)] = mm(buf[mine, :], wz_v[:, pl.ds(256, 128)]).astype(BF16)

    def taps_of(j):
        if j < tiles:
            return conv_x[:, pl.ds(j * LANES, LANES)]
        return conv_bc[:, pl.ds((j - tiles) * LANES, LANES)]

    def conv_store(j, where, val):
        if j < tiles:
            xs_s[where, pl.ds(j * LANES, LANES)] = val
        elif j == tiles:
            b_s[where, :] = val
        else:
            c_s[where, :] = val

    def conv_rows(j, source, g, start, size):
        taps = taps_of(j)
        mine = span(g, start, size)
        total = source[pl.ds(HALO - 3, size), :] * taps[0:1, :] * mask_s[0, mine, :]
        total = total + source[pl.ds(HALO - 2, size), :] * taps[1:2, :] * mask_s[1, mine, :]
        total = total + source[pl.ds(HALO - 1, size), :] * taps[2:3, :] * mask_s[2, mine, :]
        total = total + source[pl.ds(HALO, size), :] * taps[3:4, :]
        conv_store(j, mine, silu(total).astype(BF16))

    def conv_main(g, tiles_of=tuple(range(width // LANES + 2))):
        for j in tiles_of:
            cv_s[j] = xbc_s[span(g), pl.ds(j * LANES, LANES)].astype(F32)
            conv_rows(j, cv_s.at[j], g, HALO, GROUP - HALO)

    def conv_head(g, tiles_of=tuple(range(width // LANES + 2))):
        for j in tiles_of:
            cols = pl.ds(j * LANES, LANES)
            back = pl.ds(pl.multiple_of(jnp.maximum(g * GROUP - HALO, 0), HALO), HALO)

            @pl.when(g == 0)
            def _():
                cvh_s[j, pl.ds(0, HALO), :] = halo_s[:, cols].astype(F32)

            @pl.when(g > 0)
            def _():
                cvh_s[j, pl.ds(0, HALO), :] = xbc_s[back, cols].astype(F32)

            cvh_s[j, pl.ds(HALO, HALO), :] = xbc_s[span(g, 0, HALO), cols].astype(F32)
        for j in tiles_of:
            conv_rows(j, cvh_s.at[j], g, 0, HALO)

    low_ones = (
        lax.broadcasted_iota(jnp.int32, (GROUP, GROUP), 0)
        >= lax.broadcasted_iota(jnp.int32, (GROUP, GROUP), 1)
    ).astype(F32).astype(BF16)

    def steps(g):
        mine = span(g)
        raw = dt_s[mine, :] + bias_row
        dts = jnp.maximum(raw, 0.0) + jnp.log1p(jnp.exp(-jnp.abs(raw)))
        rest = -dts * rate_row
        logs = jnp.zeros((GROUP, LANES), F32)
        for _ in range(3):
            part = rest.astype(BF16)
            rest = rest - part.astype(F32)
            logs = logs + mm(low_ones, part)
        dts_s[mine, :] = dts
        logs_s[mine, :] = logs

    def documents(g):
        base = g * GROUP
        cur = segc[pl.ds(pl.multiple_of(base + HALO, 8), GROUP), :]
        return cur, segc[pl.ds(pl.multiple_of(base + HALO - 8, 8), 8), :][7:8, :]

    def state(g):
        mine = span(g)
        logs, dts = logs_s[mine, :], dts_s[mine, :]
        cur, seg_in = documents(g)
        seg_last = cur[GROUP - 1 :, :]
        final = logs[GROUP - 1 :, :]
        tail = jnp.exp(final - logs) * (cur == seg_last).astype(F32) * dts
        keep = jnp.exp(final) * (seg_last == seg_in).astype(F32)
        scaled, kept = [], []
        for p in range(tiles):
            xs = xs_s[mine, pl.ds(p * LANES, LANES)].astype(F32)
            scaled.append((xs * spread(tail, p)).astype(BF16))
            kept.append(jnp.broadcast_to(spread(keep, p), (8, LANES)))
        keep_s[g] = jnp.concatenate(kept, axis=1)
        fresh_s[g] = lax.dot_general(
            b_s[mine, :], jnp.concatenate(scaled, axis=1), (((0,), (0,)), ((), ())),
            preferred_element_type=F32,
        )

    below = lax.broadcasted_iota(jnp.int32, (LANES, LANES), 0) >= lax.broadcasted_iota(
        jnp.int32, (LANES, LANES), 1
    )
    lo, hi = slice(0, LANES), slice(LANES, GROUP)

    def mix(g):
        mine = span(g)
        cur, seg_in = documents(g)
        srow = [seg[pl.ds(g * 2 + i, 1), :].astype(F32) for i in range(2)]
        scores = lax.dot_general(
            c_s[mine, :], b_s[mine, :], (((1,), (1,)), ((), ())), preferred_element_type=F32
        )
        s00 = jnp.where(below & (cur[lo] == srow[0]), scores[lo, lo], 0.0)
        s10 = jnp.where(cur[hi] == srow[0], scores[hi, lo], 0.0)
        s11 = jnp.where(below & (cur[hi] == srow[1]), scores[hi, hi], 0.0)
        logs = logs_s[mine, :]
        lrow = jnp.transpose(logs)[0:8, :]
        drow = jnp.transpose(dts_s[mine, :])[0:8, :]
        ssm = ssm_s[...]
        high = ssm.astype(BF16)
        low = (ssm - high.astype(F32)).astype(BF16)
        cm = c_s[mine, :]
        carried = mm(cm, high) + mm(cm, low)
        enter = jnp.exp(logs) * (cur == seg_in).astype(F32)
        for p in range(tiles):
            cols = pl.ds(p * LANES, LANES)
            xs = xs_s[mine, cols]
            total = None
            for q in range(per):
                h = p * per + q
                lc = logs[:, h : h + 1]
                lr, dr = lrow[h : h + 1, :], drow[h : h + 1, :]

                def piece(s, i, j):
                    return (s * jnp.exp(jnp.minimum(lc[i] - lr[:, j], 0.0)) * dr[:, j]).astype(BF16)

                top = jnp.concatenate([piece(s00, lo, lo), jnp.zeros((LANES, LANES), BF16)], axis=1)
                bot = jnp.concatenate([piece(s10, hi, lo), piece(s11, hi, hi)], axis=1)
                part = (lane >= q * head_dim) & (lane < (q + 1) * head_dim)
                term = mm(
                    jnp.concatenate([top, bot], axis=0), jnp.where(part, xs, jnp.zeros_like(xs))
                )
                total = term if total is None else total + term
            wide = spread(enter, p)
            gate = silu(z_s[mine, cols].astype(F32))
            inside = total + carried[:, p * LANES : (p + 1) * LANES] * wide
            y_s[mine, cols] = (inside + skip_rows[p] * xs.astype(F32)) * gate
            ex_s[mine, cols] = wide * kcum_s[0:1, cols] * gate
        kept = keep_s[g]
        ssm_s[...] = ssm * kept[0:1, :] + fresh_s[g]
        kcum_s[...] = kcum_s[...] * kept

    for load in loads:
        load.wait()
    own.wait()
    m0.wait_recv()
    project_xbc(x)
    halo_if_last(x)
    project_z(x)
    conv_main(x)
    steps(x)
    a_r0.wait_recv()
    a_l1.wait_recv()
    for copy in relay_r + relay_l + [fwd_l0, fwd_r1]:
        copy.start()
    fwd_l0.wait_recv()
    project_some(xl, halves[0])
    project_z_some(xl, halves[0])
    fwd_r1.wait_recv()
    project_some(xr, halves[1])
    halo_if_last(xr)
    project_z_some(xr, halves[1])
    a_r1.wait_recv()
    fwd_l1.start()
    a_l0.wait_recv()
    fwd_r0.start()
    fwd_l1.wait_recv()
    project_some(xl, halves[1])
    halo_if_last(xl)
    fwd_r0.wait_recv()
    project_some(xr, halves[0])
    relay_r[0].wait_recv()
    fwd_f[0][0].start()
    relay_l[0].wait_recv()
    fwd_f[0][1].start()
    conv_main(xl)
    steps(xl)
    conv_main(xr)
    steps(xr)

    def halo_wait(places):
        @pl.when(places & inner)
        def _():
            to_halo.wait_recv()

    halo_wait((x == 0) | (x == nx - 1))

    conv_head(xr)
    relay_r[1].wait_recv()
    fwd_f[1][0].start()
    relay_l[1].wait_recv()
    fwd_f[1][1].start()
    state(xr)
    conv_head(x)
    state(x)
    for slices, pair in zip(quarters, fwd_f):
        for copy in pair:
            copy.wait_recv()
        project_some(xf, slices)
    halo_if_last(xf)
    conv_main(xf, tuple(range(tiles + 1)))
    steps(xf)
    halo_wait(x == 2)
    conv_head(xf, tuple(range(tiles + 1)))
    state(xf)
    halo_wait(x == 1)
    conv_head(xl, tuple(range(tiles + 1)))
    state(xl)

    hops = [
        [remote(hop_out.at[h, p], hop_in.at[h, p], after) for p in range(tiles)]
        for h in range(HOPS)
    ]
    for p in range(tiles):
        cols = pl.ds(p * LANES, LANES)
        total, decay = fresh_s[0, :, cols], keep_s[0, :, cols]
        for g in range(1, nx):
            total = total * keep_s[g, 0:1, cols] + fresh_s[g, :, cols]
            decay = decay * keep_s[g, :, cols]
        local_s[:, cols] = total
        decay_s[:, cols] = decay
        hop_out[0, p] = total.astype(BF16)
        when_outer(hops[0][p].start)

    def hop_on(h):
        for p in range(tiles):
            cols = pl.ds(p * LANES, LANES)
            when_inner(hops[h - 1][p].wait_recv)
            total = local_s[:, cols] + decay_s[0:1, cols] * hop_in[h - 1, p].astype(F32)
            hop_out[h, p] = total.astype(BF16)
            when_outer(hops[h][p].start)

    ssm_s[...] = jnp.zeros_like(ssm_s)
    kcum_s[...] = jnp.ones_like(kcum_s)

    def mix_step(g, carry):
        mix(g)
        return carry

    conv_main(xf, (tiles + 1,))
    conv_head(xf, (tiles + 1,))
    conv_head(xl, (tiles + 1,))
    project_z_some(xr, halves[0])
    project_z_some(xl, halves[1])
    project_z(xf)
    lax.fori_loop(0, 1, mix_step, 0)
    hop_on(1)
    lax.fori_loop(1, 2, mix_step, 0)
    hop_on(2)
    lax.fori_loop(2, nx, mix_step, 0)
    load_wo.wait()
    to_wo.wait_recv()
    for p in range(tiles):
        when_inner(hops[HOPS - 1][p].wait_recv)
        enter_s[:, pl.ds(p * LANES, LANES)] = hop_in[HOPS - 1, p]

    eye = (
        lax.broadcasted_iota(jnp.int32, (LANES, LANES), 0)
        == lax.broadcasted_iota(jnp.int32, (LANES, LANES), 1)
    )
    order = (2, 1, -1, 0)
    swaps = []
    for k in order:
        to = pl.ds(pl.multiple_of(rot(k) * rows, rows), rows)
        swaps.append(
            remote(g_s.at[1, to, pl.ds(0, width)], g_s.at[0, to, pl.ds(width, width)], mate)
        )

    def finish(k, swap):
        g = rot(k)
        for side in (1, 0):
            i = lax.rem(c + side, 2)
            mine = span(g, i * LANES, LANES)
            to = pl.ds(pl.multiple_of(g * rows, rows), rows)
            carried = mm(c_s[mine, :], enter_s[...])
            squares = jnp.zeros((LANES, LANES), F32)
            for p in range(tiles):
                cols = pl.ds(p * LANES, LANES)
                val = y_s[mine, cols] + carried[:, p * LANES : (p + 1) * LANES] * ex_s[mine, cols]
                squares = squares + val * val
                g_s[side, to, cols] = (val * gain[:, p * LANES : (p + 1) * LANES]).astype(BF16)
            sums = jnp.sum(squares, axis=1, keepdims=True)
            row = jnp.sum(jnp.where(eye, sums, 0.0), axis=0, keepdims=True)
            ss_s[g * 2 + i] = jnp.broadcast_to(row, (8, LANES))
            if side == 1:
                swap.start()

    spans = [pl.ds(i * PIECE, PIECE) for i in range(depth // PIECE)]
    bounds = [len(spans) * i // PARTS for i in range(PARTS + 1)]
    parts = [spans[i:j] for i, j in zip(bounds, bounds[1:])]
    part_cols = [pl.ds(i * PIECE, (j - i) * PIECE) for i, j in zip(bounds, bounds[1:])]

    def product(k, cols):
        mine = pl.ds(pl.multiple_of(rot(k) * rows, rows), rows)
        return mm(g_s[0, mine, :], wo_v[:, cols])

    far = [
        (remote(to_r.at[:, cols], far_r.at[:, cols], right), remote(to_l.at[:, cols], far_l.at[:, cols], left))
        for cols in part_cols
    ]
    plain_r = remote(near_r.at[1], from_l.at[1], right)
    plain_l = remote(near_l.at[0], from_r.at[0], left)
    merged = [
        (
            remote(near_r.at[0, :, cols], from_l.at[0, :, cols], right),
            remote(near_l.at[1, :, cols], from_r.at[1, :, cols], left),
        )
        for cols in part_cols
    ]
    finish(2, swaps[0])
    finish(1, swaps[1])
    swaps[0].wait_recv()
    for part, pair in zip(parts, far):
        for cols in part:
            v = product(2, cols).astype(BF16)
            to_r[:, cols] = v[:half]
            to_l[:, cols] = v[half:]
        pair[0].start()
        pair[1].start()
    finish(-1, swaps[2])
    finish(0, swaps[3])
    sums = []
    for k in range(1, n):
        copy = remote(ss_s.at[lax.rem(w + k, n)], ss_in.at[w], others[k - 1])
        copy.start()
        sums.append(copy)
    swaps[1].wait_recv()
    for cols in spans:
        v = product(1, cols)
        keep_r[:, cols] = v[:half]
        near_r[1, :, cols] = v[half:].astype(BF16)
    plain_r.start()
    swaps[2].wait_recv()
    for cols in spans:
        v = product(-1, cols)
        near_l[0, :, cols] = v[:half].astype(BF16)
        keep_l[:, cols] = v[half:]
    plain_l.start()
    swaps[3].wait_recv()
    for cols in spans:
        acc[:, cols] = product(0, cols)
    for part, pair, ready in zip(parts, far, merged):
        pair[0].wait_recv()
        for cols in part:
            near_r[0, :, cols] = (keep_r[:, cols] + far_r[:, cols].astype(F32)).astype(BF16)
        ready[0].start()
        pair[1].wait_recv()
        for cols in part:
            near_l[1, :, cols] = (keep_l[:, cols] + far_l[:, cols].astype(F32)).astype(BF16)
        ready[1].start()
    for copy in sums:
        copy.wait_recv()
    ss_in[w] = ss_s[w]
    square = jnp.sum(ss_in[...], axis=0)[0:1, :]
    inverse = lax.rsqrt(square / (width * n) + EPS)
    scale = jnp.sum(jnp.where(eye, inverse, 0.0), axis=1, keepdims=True)
    plain_r.wait_recv()
    plain_l.wait_recv()
    for cols in spans:
        acc[hi_half, cols] = acc[hi_half, cols] + from_l[1, :, cols].astype(F32)
        acc[lo_half, cols] = acc[lo_half, cols] + from_r[0, :, cols].astype(F32)
    stores = [
        pltpu.make_async_copy(out.at[:, cols], out_h.at[:, cols], local.at[13 + i])
        for i, cols in enumerate(part_cols)
    ]
    for i, (part, pair) in enumerate(zip(parts, merged)):
        pair[0].wait_recv()
        pair[1].wait_recv()
        for cols in part:
            v = acc[lo_half, cols] + from_l[0, :, cols].astype(F32)
            out[lo_half, cols] = (v * scale[:half]).astype(BF16)
            v = acc[hi_half, cols] + from_r[1, :, cols].astype(F32)
            out[hi_half, cols] = (v * scale[half:]).astype(BF16)
        stores[i].start()
    assert len(copies) <= COPIES
    along = [to_seg, to_halo] + [hop for row in hops for hop in row]
    for copy in copies:
        if all(copy is not other for other in along):
            copy.wait_send()

    @pl.when(outer)
    def _():
        for copy in along:
            copy.wait_send()

    for store in stores:
        store.wait()


def on_device(
    tokens, segments, w_z, w_x, w_dt, w_bc, conv_x, conv_bc, dt_bias, decay_rate, skip_d,
    norm_gain, w_out,
):
    n = lax.axis_size("weight")
    nx, nt = n // 2, lax.axis_size("tm")
    seg = segments.reshape(-1, LANES)
    rows, depth = tokens.shape
    width, heads = w_z.shape[1], decay_rate.shape[0]
    block, half = rows * n, rows // 2
    tiles = width // LANES
    wide = width + w_bc.shape[1]
    count = block // GROUP
    hbm = whole(pl.ANY)
    V = pltpu.VMEM
    return pl.pallas_call(
        functools.partial(layer_kernel, nx, nt, heads),
        out_shape=jax.ShapeDtypeStruct((rows, depth), BF16),
        in_specs=[whole(pltpu.HBM)] * 13,
        out_specs=hbm,
        scratch_shapes=[
            V(seg.shape, jnp.int32),
            V((heads, depth), BF16),
            V(conv_x.shape, F32),
            V(conv_bc.shape, F32),
            V((width,), BF16),
            pltpu.SMEM((heads,), F32),
            pltpu.SMEM((heads,), F32),
            pltpu.SMEM((heads,), F32),
            V((rows, depth), BF16),
            V((block, depth), BF16),
            V((depth, wide + LANES), BF16),
            V((depth, width), BF16),
            V((8, depth), F32),
            V((2 * width, depth), BF16),
            V((block, width), BF16),
            V((block, wide), BF16),
            V((block, LANES), F32),
            V((HALO, wide), BF16),
            V(seg.shape, jnp.int32),
            V((block + HALO, LANES), F32),
            V((3, block, LANES), F32),
            V((tiles + 2, GROUP, LANES), F32),
            V((tiles + 2, 2 * HALO, LANES), F32),
            V((block, width), BF16),
            V((block, LANES), BF16),
            V((block, LANES), BF16),
            V((block, LANES), F32),
            V((block, LANES), F32),
            V((count, LANES, width), F32),
            V((count, 8, width), F32),
            V((block, width), F32),
            V((block, width), F32),
            V((LANES, width), F32),
            V((8, width), F32),
            V((LANES, width), F32),
            V((8, width), F32),
            V((HOPS, tiles, LANES, LANES), BF16),
            V((HOPS, tiles, LANES, LANES), BF16),
            V((LANES, width), BF16),
            V((2, nx * rows, 2 * width), BF16),
            V((n, 8, LANES), F32),
            V((n, 8, LANES), F32),
            V((half, depth), BF16),
            V((half, depth), BF16),
            V((half, depth), BF16),
            V((half, depth), BF16),
            V((2, half, depth), BF16),
            V((2, half, depth), BF16),
            V((2, half, depth), BF16),
            V((2, half, depth), BF16),
            V((half, depth), F32),
            V((half, depth), F32),
            V((rows, depth), F32),
            pltpu.SemaphoreType.DMA((COPIES,)),
            pltpu.SemaphoreType.DMA((COPIES,)),
            pltpu.SemaphoreType.DMA((13 + PARTS,)),
            pltpu.SemaphoreType.REGULAR,
        ],
        compiler_params=pltpu.CompilerParams(
            collective_id=0, has_side_effects=True, vmem_limit_bytes=VMEM_LIMIT
        ),
        name="layer_block",
    )(
        tokens, seg, w_z, w_x, w_bc, w_dt.T, conv_x, conv_bc, norm_gain, w_out,
        dt_bias, decay_rate, skip_d,
    )


def solution(mesh):
    return jax.shard_map(
        on_device,
        mesh=mesh,
        in_specs=(
            P(("tm", "weight"), None),
            P("tm"),
            P(None, "weight"),
            P(None, "weight"),
            P(None, "weight"),
            P(),
            P(None, "weight"),
            P(),
            P("weight"),
            P("weight"),
            P("weight"),
            P("weight"),
            P("weight", None),
        ),
        out_specs=P(("tm", "weight"), None),
        check_vma=False,
    )
```
